32 devices in a mesh: gx: 2 (over x), gy: 4 (over y, core), gz: 4 (over z).
Axes of the slice: x: 2, y: 2, z: 4, core: 2. Of those that a mesh axis runs over, the one named last changes fastest.
Arguments:
- solution_in: float32 [16, 128, 512], P('gx', 'gy', 'gz'), may hold values from -6 to 6
- residual_in: float32 [16, 128, 512], P('gx', 'gy', 'gz'), may hold values from -12 to 12
- direction_in: float32 [16, 128, 512], P('gx', 'gy', 'gz'), may hold values from -6 to 6
- material: int32 [16, 128, 512], P('gx', 'gy', 'gz'), may hold values from 0 to 7
- cond_table: float32 [8], replicated, may hold values from 0.5 to 4
- cap_table: float32 [8], replicated, may hold values from 0.2 to 1
- gas_flux: float32 [128, 512], P('gy', 'gz'), may hold values from -6 to 6
- supply_map: int32 [128, 512], P('gy', 'gz'), may hold values from 0 to 511, as said below
Outputs:
- solution: float32 [16, 128, 512], P('gx', 'gy', 'gz')
- residual: float32 [16, 128, 512], P('gx', 'gy', 'gz')
- direction: float32 [16, 128, 512], P('gx', 'gy', 'gz')
The draws below stay inside these ranges and needn't reach their ends.
Inputs may be any that keep to these rules, and one draw needn't show every extreme that they name: `supply_map`: the gas faces are laid out so that the faces held by index q of gz, in their slots t * 128 / 4 to (t + 1) * 128 / 4 - 1, supply solid faces held by index t of gz in the same row; every gas face supplies exactly one solid face of its row.
All inputs are finite; a program needn't handle non-finite values.
Results may differ from the reference program's by a relative error of at most 0.0006.
Values sent between devices are 32-bit elements; how exact they have to be, the bound alone decides.
A program may use at most 64 MiB of HBM per device.

```python
import math
import jax
import jax.numpy as jnp
from jax import lax

CZ = 128
STEPS = 4
MATERIALS = 8
NX = 16
NY = 128
NZ = 512


def draw_residual_in(key, part):
    depth = jnp.arange(NX, dtype=jnp.float32) / NX
    scaling = (0.5 + 1.5 * depth)[:, None, None]
    base = jax.random.truncated_normal(key, -6.0, 6.0, (NX, NY, NZ), jnp.float32)
    return base * scaling


def draw_supply_map(key, part):
    groups = NZ // CZ
    segment = CZ // groups
    keys = jax.random.split(jax.random.fold_in(key, 7), NY * groups)
    orders = jax.vmap(lambda single: jax.random.permutation(single, CZ))(keys).astype(jnp.int32)
    orders = orders.reshape(NY, groups, CZ)
    target = jnp.arange(groups, dtype=jnp.int32)[None, :, None]
    mapped = orders // segment * CZ + target * segment + orders % segment
    return mapped.reshape(NY, NZ).astype(jnp.int32)


def touch_ends(array, rng, low, high):
    longest = array.shape.index(max(array.shape))
    spots = []
    for shift in (0, 1):
        where = [jax.random.randint(jax.random.fold_in(rng, axis), (), 0, length) for axis, length in enumerate(array.shape)]
        where[longest] = (where[longest] + shift) % array.shape[longest]
        spots.append(tuple(where))
    return array.at[spots[0]].set(low).at[spots[1]].set(high)


def block_levels(stream_key, dims, pieces, least, high):
    level, own = 1.0, jax.random.fold_in(stream_key, 6)
    for dim, parts in pieces:
        steps = jnp.exp(jax.random.uniform(jax.random.fold_in(own, dim), (parts,), jnp.float32, least / len(pieces), high / len(pieces)))
        level = level * jnp.repeat(steps, dims[dim] // parts).reshape([-1 if axis == dim else 1 for axis in range(len(dims))])
    return level


def normal_values(stream_key, shape, scale, limit, cuts=(), kind=jnp.bfloat16):
    values = scale * jax.random.normal(stream_key, shape, jnp.float32)
    if cuts:
        values = values * block_levels(stream_key, shape, cuts, -0.22, 0.18)
    return jnp.clip(values, -limit, limit).astype(kind)


def setup_inputs(seed: int = 0) -> dict:
    arg_keys = jax.random.split(jax.random.key(seed), 9)
    solution_in = normal_values(arg_keys[0], (NX, NY, NZ), 1.0, 6.0, ((0, 2), (1, 4), (2, 4)), jnp.float32)
    residual_in = draw_residual_in(jax.random.fold_in(arg_keys[8], 71), 0)
    direction_in = normal_values(arg_keys[2], (NX, NY, NZ), 1.0, 6.0, ((0, 2), (1, 4), (2, 4)), jnp.float32)
    material = touch_ends(jax.random.randint(arg_keys[3], (NX, NY, NZ), 0, MATERIALS), jax.random.fold_in(arg_keys[3], 1), 0, MATERIALS - 1).astype(jnp.int32)
    cond_table = jnp.clip(jnp.exp(jax.random.uniform(arg_keys[4], (MATERIALS,), jnp.float32, math.log(0.5), math.log(4.0))), 0.5, 4.0)
    cap_table = jnp.clip(jnp.exp(jax.random.uniform(arg_keys[5], (MATERIALS,), jnp.float32, math.log(0.2), math.log(1.0))), 0.2, 1.0)
    gas_flux = normal_values(arg_keys[6], (NY, NZ), 1.0, 6.0, ((0, 4), (1, 4)), jnp.float32)
    supply_map = draw_supply_map(jax.random.fold_in(arg_keys[8], 71), 0)
    return dict(solution_in=solution_in, residual_in=residual_in, direction_in=direction_in, material=material, cond_table=cond_table, cap_table=cap_table, gas_flux=gas_flux, supply_map=supply_map)


def harmonic(lower_side, upper_side):
    return 2.0 * lower_side * upper_side / (jnp.where(lower_side > 0, lower_side, 1.0) + jnp.where(upper_side > 0, upper_side, 1.0))


def face_terms(cond):
    return (harmonic(cond[:-1], cond[1:]), harmonic(cond[:, :-1], cond[:, 1:]), harmonic(cond[:, :, :-1], cond[:, :, 1:]))


def operate(values, capacity, conductance):
    result = capacity * values
    face_flow = conductance[0] * (values[1:] - values[:-1])
    result = result - jnp.pad(face_flow, ((0, 1), (0, 0), (0, 0))) + jnp.pad(face_flow, ((1, 0), (0, 0), (0, 0)))
    face_flow = conductance[1] * (values[:, 1:] - values[:, :-1])
    result = result - jnp.pad(face_flow, ((0, 0), (0, 1), (0, 0))) + jnp.pad(face_flow, ((0, 0), (1, 0), (0, 0)))
    face_flow = conductance[2] * (values[:, :, 1:] - values[:, :, :-1])
    result = result - jnp.pad(face_flow, ((0, 0), (0, 0), (0, 1))) + jnp.pad(face_flow, ((0, 0), (0, 0), (1, 0)))
    return result


def lookup(material, table):
    summed = jnp.zeros(material.shape, jnp.float32)
    for material_id in range(table.shape[0]):
        summed = summed + jnp.where(material == material_id, table[material_id], jnp.float32(0.0))
    return summed


def spectrum(cond_table, cap_table):
    lowest = jnp.min(cap_table)
    highest = jnp.max(cap_table) + 12.0 * jnp.max(cond_table)
    return 0.5 * (highest + lowest), 0.5 * (highest - lowest)


def next_term(applied, terms, center, half_width):
    shifted = (applied - center * terms[-1]) / half_width
    if len(terms) == 1:
        return shifted
    return 2.0 * shifted - terms[-2]


def chebyshev(values, degree, capacity, conductance, center, half_width):
    terms = [values]
    for sweep in range(degree):
        terms.append(next_term(operate(terms[-1], capacity, conductance), terms, center, half_width))
    return terms


def shift_matrix(center, half_width, steps):
    dimension = 2 * steps + 1
    matrix = jnp.zeros((dimension, dimension), jnp.float32)
    for offset, length in ((0, steps + 1), (steps + 1, steps)):
        for column in range(length - 1):
            matrix = matrix.at[offset + column, offset + column].set(center)
            matrix = matrix.at[offset + column + 1, offset + column].set(half_width if column == 0 else 0.5 * half_width)
            if column >= 1:
                matrix = matrix.at[offset + column - 1, offset + column].set(0.5 * half_width)
    return matrix


def coefficients(gram, center, half_width, steps):
    dimension = 2 * steps + 1
    matrix = shift_matrix(center, half_width, steps)
    highest_prec = lax.Precision.HIGHEST

    def gram_product(first_vec, second_vec):
        return jnp.dot(first_vec, jnp.dot(gram, second_vec, precision=highest_prec), precision=highest_prec)

    direct = jnp.zeros((dimension,), jnp.float32).at[0].set(1.0)
    residue = jnp.zeros((dimension,), jnp.float32).at[steps + 1].set(1.0)
    moved = jnp.zeros((dimension,), jnp.float32)
    norm_now = gram_product(residue, residue)
    for sweep in range(steps):
        mapped = jnp.dot(matrix, direct, precision=highest_prec)
        step_length = norm_now / gram_product(direct, mapped)
        moved = moved + step_length * direct
        residue = residue - step_length * mapped
        norm_next = gram_product(residue, residue)
        direct = residue + (norm_next / norm_now) * direct
        norm_now = norm_next
    return moved, residue, direct


def combine(weights, basis):
    summed = weights[0] * basis[0]
    for position in range(1, len(basis)):
        summed = summed + weights[position] * basis[position]
    return summed


def reference(solution_in, residual_in, direction_in, material, cond_table, cap_table, gas_flux, supply_map):
    incoming = jnp.take_along_axis(gas_flux, supply_map, axis=1)
    start = residual_in.at[NX - 1].add(incoming)
    conductance = face_terms(lookup(material, cond_table))
    capacity = lookup(material, cap_table)
    center, half_width = spectrum(cond_table, cap_table)
    basis = chebyshev(direction_in, STEPS, capacity, conductance, center, half_width)
    basis = basis + chebyshev(start, STEPS - 1, capacity, conductance, center, half_width)
    dimension = len(basis)
    rows_list = []
    for first_id in range(dimension):
        entries = []
        for second_id in range(dimension):
            entries.append(jnp.sum(basis[first_id] * basis[second_id]))
        rows_list.append(jnp.stack(entries))
    gram = jnp.stack(rows_list)
    moved, residue, direct = coefficients(gram, center, half_width, STEPS)
    return (solution_in + combine(moved, basis), combine(residue, basis), combine(direct, basis))
```

```python
import jax
import jax.numpy as jnp
from jax import lax
from jax.experimental import pallas as pl
from jax.experimental.pallas import tpu as pltpu
from jax.sharding import PartitionSpec as P

STEPS = 4
VMEM = 63 * 1024 * 1024
AXES = ("gx", "gy", "gz")
MESH = pl.DeviceIdType.MESH
DIM = 2 * STEPS + 1
PAIRS = [(i, j) for i in range(DIM) for j in range(i, DIM)]
SLOT = {pair: k for k, pair in enumerate(PAIRS)}


def harmonic(a, b):
    return 2.0 * a * b / jnp.maximum(a + b, 1e-30)


def tree(parts):
    while len(parts) > 1:
        parts = [sum(parts[k:k + 2][1:], parts[k]) for k in range(0, len(parts), 2)]
    return parts[0]


def times(a, b):
    return None if a is None or b is None else a * b


def plus(a, b):
    return b if a is None else a if b is None else a + b


def shift_product(p, center, half_width):
    q = [None] * DIM
    for offset, length in ((0, STEPS + 1), (STEPS + 1, STEPS)):
        for column in range(length - 1):
            entry = p[offset + column]
            if entry is None:
                continue
            q[offset + column] = plus(q[offset + column], center * entry)
            low = half_width if column == 0 else 0.5 * half_width
            q[offset + column + 1] = plus(q[offset + column + 1], low * entry)
            if column >= 1:
                q[offset + column - 1] = plus(q[offset + column - 1], 0.5 * half_width * entry)
    return q


def form(gram, a, b):
    total = None
    for i in range(DIM):
        if a[i] is None:
            continue
        row = None
        for j in range(DIM):
            row = plus(row, times(gram[i][j], b[j]))
        total = plus(total, a[i] * row)
    return total


def coefficients(gram, center, half_width):
    one = jnp.ones_like(gram[0][0])
    p = [None] * DIM
    r = [None] * DIM
    x = [None] * DIM
    p[0] = one
    r[STEPS + 1] = one
    rr = form(gram, r, r)
    for _ in range(STEPS):
        q = shift_product(p, center, half_width)
        step = rr / form(gram, p, q)
        x = [plus(x[i], times(step, p[i])) for i in range(DIM)]
        r = [plus(r[i], times(-step, q[i])) for i in range(DIM)]
        new = form(gram, r, r)
        ratio = new / rr
        p = [plus(r[i], times(ratio, p[i])) for i in range(DIM)]
        rr = new
    return x, r, p


MAT, D0, S0 = 0, 1, 2
TERMS = [D0, 3, 4, 5, 6, S0, 7, 8, 9]
FIELDS = 10


def both(*conditions):
    kept = [c for c in conditions if c is not True]
    if not kept:
        return True
    total = kept[0]
    for c in kept[1:]:
        total = jnp.logical_and(total, c)
    return total


def guard(condition, action):
    if condition is True:
        action()
    else:
        pl.when(condition)(action)


def layout(gx, count):
    if count == 2:
        own = 4 * gx
        sides = [dict(
            peer=1 - gx, send=True, recv=True, strip=4, ghost=8 * (1 - gx),
            src4=4, dst4=8 * gx, in4=8 * (1 - gx),
            src3=5 - gx, dst3=1 + 7 * gx, in3=1 + 7 * (1 - gx),
        )]
        return 12, own, sides
    own = 4
    sides = [
        dict(peer=gx - 1, send=gx > 0, recv=gx < count - 1, strip=4, ghost=12,
             src4=4, dst4=12, in4=12, src3=4, dst3=12, in3=12),
        dict(peer=gx + 1, send=gx < count - 1, recv=gx > 0, strip=8, ghost=0,
             src4=8, dst4=0, in4=0, src3=9, dst3=1, in3=1),
    ]
    return 16, own, sides


def message_count(sizes):
    sides = 1 if sizes["gx"] == 2 else 2
    return 8 + sides * 10


def kernel(
    sizes, stages, cond_in, cap_in, sol_in, res_in, dir_in, mat_in, gas_in, map_in,
    sol_out, res_out, dir_out,
    fields, strip, held, cond_tab, cap_tab, mat_ref, flux, map_ref,
    condm, diag, kx, ky, kzl, kzh, conds, sdiag, sk, sy,
    pack, corner, strip_in, corner_in, gram_send, gram_halo,
    send_sem, recv_sem, flux_ssem, flux_rsem, map_ssem, map_rsem,
    gram_ssem, gram_rsem, load_sem, store_sem, known_a, known_b,
):
    pos = {axis: lax.axis_index(axis) for axis in AXES}
    gx, gy, gz = (pos[axis] for axis in AXES)
    nx, ny, nz = (sizes[axis] for axis in AXES)
    slots, own, sides = layout(gx, nx)
    is_top = gx == nx - 1
    lane = lax.broadcasted_iota(jnp.int32, (8, 128), 1)
    group = lane // 8
    inner = lax.rem(lane, 8)
    own1 = own + 1

    loads = []
    for source, target in (
        (mat_in, mat_ref),
        (dir_in, fields.at[D0, pl.ds(own1, 8), pl.ds(8, 32)]),
        (res_in, fields.at[S0, pl.ds(own1, 8), pl.ds(8, 32)]),
        (map_in, map_ref.at[pl.ds(8, 32)]),
        (gas_in, flux.at[gz, pl.ds(8, 32)]),
        (cond_in, cond_tab), (cap_in, cap_tab),
        (sol_in, held.at[0]),
    ):
        loads.append(pltpu.make_async_copy(source, target, load_sem.at[len(loads)]))
        loads[-1].start()

    barrier = pltpu.get_barrier_semaphore()
    count = jnp.int32(0)

    def inside(axis, step):
        if step == 0:
            return True
        return pos[axis] > 0 if step < 0 else pos[axis] < sizes[axis] - 1

    def greet(condition, peer):
        nonlocal count
        guard(condition, lambda: pl.semaphore_signal(barrier, inc=1, device_id=peer, device_id_type=MESH))
        count = count + (1 if condition is True else jnp.where(condition, 1, 0))

    def along(axis):
        return [lax.rem(pos[axis] + o, sizes[axis]) for o in range(1, sizes[axis])]

    for axis in AXES:
        for where in along(axis):
            greet(True, {axis: where})
    for dy in (-1, 1):
        for z in along("gz"):
            near = jnp.logical_or(jnp.abs(z - gz) == 1, is_top)
            greet(both(inside("gy", dy), near), {"gy": gy + dy, "gz": z})
    for side in sides:
        for dy in (-1, 0, 1):
            for dz in (-1, 0, 1):
                if dy or dz:
                    greet(
                        both(side["send"], inside("gy", dy), inside("gz", dz)),
                        {"gx": side["peer"], "gy": gy + dy, "gz": gz + dz},
                    )

    def blank(condition, slot_start, slot_count, rows):
        def fill():
            for f, value in ((MAT, -1.0), (D0, 0.0), (S0, 0.0)):
                fields[f, pl.ds(slot_start, slot_count), rows, :] = jnp.full(
                    (slot_count, rows.stop - rows.start, 128), value, jnp.float32
                )
        guard(condition, fill)

    low_rows, high_rows = slice(0, 8), slice(40, 48)
    blank(gy == 0, 1, slots, low_rows)
    blank(gy == ny - 1, 1, slots, high_rows)
    for side in sides:
        if side["recv"] is not True:
            blank(jnp.logical_not(side["recv"]), side["in4"] + 1, 4, slice(0, 48))
    zeros48 = jnp.zeros((48, 128), jnp.float32)
    for f in range(FIELDS):
        fields[f, 0] = zeros48
        fields[f, slots + 1] = zeros48
    condm[0] = zeros48
    condm[slots + 1] = zeros48

    def blank_strip(condition, dz_index, rows):
        def fill():
            for k in rows:
                strip_in[dz_index, 0, k] = jnp.full((8, 128), -1.0, jnp.float32)
                for f in range(1, 4):
                    strip_in[dz_index, f, k] = jnp.zeros((8, 128), jnp.float32)
        guard(condition, fill)

    def blank_corner(condition, x_index, dz_index, rows):
        def fill():
            for k in rows:
                corner_in[x_index, dz_index, k] = jnp.where(lane < 32, -1.0, 0.0)
        guard(condition, fill)

    for dz_index, alone in ((0, gz == 0), (1, gz == nz - 1)):
        blank_strip(alone, dz_index, range(6))
        blank_strip(gy == 0, dz_index, [0])
        blank_strip(gy == ny - 1, dz_index, [5])
        for x_index, side in enumerate(sides):
            blank_corner(alone, x_index, dz_index, range(6))
            blank_corner(gy == 0, x_index, dz_index, [0])
            blank_corner(gy == ny - 1, x_index, dz_index, [5])
            if side["recv"] is not True:
                blank_corner(jnp.logical_not(side["recv"]), x_index, dz_index, range(6))

    def blank_flux(condition, rows):
        def fill():
            flux[:, rows, :] = jnp.zeros((nz, 8, 128), jnp.float32)
            map_ref[rows, :] = jnp.zeros((8, 128), jnp.int32)
        guard(condition, fill)

    blank_flux(gy == 0, low_rows)
    blank_flux(gy == ny - 1, high_rows)

    loads[0].wait()
    fields[MAT, pl.ds(own1, 8), pl.ds(8, 32), :] = mat_ref[...].astype(jnp.float32)
    loads[1].wait()
    loads[2].wait()
    loads[3].wait()
    mirrored = lane + 7 - 2 * inner

    def place(tile):
        if nx == 2:
            tile = jnp.where(gx == 1, pltpu.roll(tile, 32, axis=1), tile)
        else:
            tile = pltpu.roll(tile, 32, axis=1)
        return jnp.take_along_axis(tile, mirrored, axis=1)

    for k in range(4):
        rows = slice(8 + 8 * k, 16 + 8 * k)
        for f in range(3):
            tile = jnp.full((8, 128), -1.0 if f == MAT else 0.0, jnp.float32)
            for i in range(8):
                moved = pltpu.roll(fields[f, own1 + i, rows, :], 8 * i + 4, axis=1)
                tile = jnp.where(group == i, moved, tile)
            pack[f, k] = place(tile)
        moved = pltpu.roll(map_ref[rows, :].astype(jnp.float32), 8 * 7 + 4, axis=1)
        pack[3, k] = place(jnp.where(group == 7, moved, 0.0))
        for x_index, side in enumerate(sides):
            tile = jnp.zeros((8, 128), jnp.float32)
            for f in range(3):
                amount = (32 * f - 8 * side["strip"]) % 128
                moved = pltpu.roll(pack[f, k], amount, axis=1) if amount else pack[f, k]
                tile = jnp.where(lane // 32 == f, moved, tile)
            corner[x_index, k] = tile
    loads[4].wait()

    messages = []
    for x_index, side in [(None, None)] + list(enumerate(sides)):
        for dy in (-1, 0, 1):
            for dz in (-1, 0, 1):
                if side is None and not dy and not dz:
                    continue
                sends = both(inside("gy", dy), inside("gz", dz))
                takes = both(inside("gy", -dy), inside("gz", -dz))
                peer = {}
                if dy:
                    peer["gy"] = gy + dy
                if dz:
                    peer["gz"] = gz + dz
                if side is not None:
                    sends = both(sends, side["send"])
                    takes = both(takes, side["recv"])
                    peer["gx"] = side["peer"]
                row_from = pl.ds(8, 32) if not dy else pl.ds(32, 8) if dy > 0 else pl.ds(8, 8)
                row_to = pl.ds(8, 32) if not dy else pl.ds(0, 8) if dy > 0 else pl.ds(40, 8)
                tile_from = pl.ds(0, 4) if not dy else pl.ds(3, 1) if dy > 0 else pl.ds(0, 1)
                tile_to = pl.ds(1, 4) if not dy else pl.ds(0, 1) if dy > 0 else pl.ds(5, 1)
                came = 0 if dz > 0 else 1
                if side is None and not dz:
                    parts = [(
                        fields.at[pl.ds(0, 3), pl.ds(own1, 8), row_from],
                        fields.at[pl.ds(0, 3), pl.ds(own1, 8), row_to],
                        fields.at[pl.ds(0, 3), pl.ds(own1, 8), row_to],
                    )]
                elif side is None:
                    target = strip_in.at[came, :, tile_to]
                    parts = [(pack.at[:, tile_from], target, target)]
                elif dz:
                    target = corner_in.at[x_index, came, tile_to]
                    parts = [(corner.at[x_index, tile_from], target, target)]
                elif dy:
                    parts = [tuple(
                        fields.at[pl.ds(0, 3), pl.ds(side[name] + 1, 3), rows]
                        for name, rows in (("src3", row_from), ("dst3", row_to), ("in3", row_to))
                    )]
                else:
                    parts = [tuple(
                        fields.at[pl.ds(0, 2), pl.ds(side[name] + 1, 4), row_from]
                        for name in ("src4", "dst4", "in4")
                    ), tuple(
                        fields.at[S0, pl.ds(side[name] + 1, 3), row_from]
                        for name in ("src3", "dst3", "in3")
                    )]
                for source, target, landing in parts:
                    number = len(messages)
                    messages.append(dict(
                        sends=sends, takes=takes, kind=(x_index, dy, dz),
                        copy=pltpu.make_async_remote_copy(
                            src_ref=source, dst_ref=target,
                            send_sem=send_sem.at[number], recv_sem=recv_sem.at[number],
                            device_id=peer, device_id_type=MESH,
                        ),
                        landed=pltpu.make_async_remote_copy(
                            src_ref=landing, dst_ref=landing,
                            send_sem=send_sem.at[number], recv_sem=recv_sem.at[number],
                            device_id=peer, device_id_type=MESH,
                        ),
                    ))

    wall = []
    for kind, dy in enumerate((0, -1, 1)):
        row_from = pl.ds(8, 32) if not dy else pl.ds(32, 8) if dy > 0 else pl.ds(8, 8)
        row_to = pl.ds(8, 32) if not dy else pl.ds(0, 8) if dy > 0 else pl.ds(40, 8)
        sends = both(is_top, inside("gy", dy))
        takes = both(is_top, inside("gy", -dy))
        if dy:
            wall.append(dict(
                sends=sends, takes=takes,
                copy=pltpu.make_async_remote_copy(
                    src_ref=map_ref.at[row_from], dst_ref=map_ref.at[row_to],
                    send_sem=map_ssem.at[kind - 1], recv_sem=map_rsem.at[kind - 1],
                    device_id={"gy": gy + dy}, device_id_type=MESH,
                ),
                landed=pltpu.make_async_remote_copy(
                    src_ref=map_ref.at[row_to], dst_ref=map_ref.at[row_to],
                    send_sem=map_ssem.at[kind - 1], recv_sem=map_rsem.at[kind - 1],
                    device_id={"gy": gy - dy}, device_id_type=MESH,
                ),
            ))
        for o in range(nz):
            if not dy and not o:
                continue
            z = lax.rem(gz + o, nz)
            peer = {"gy": gy + dy, "gz": z}
            wall.append(dict(
                sends=sends, takes=takes,
                copy=pltpu.make_async_remote_copy(
                    src_ref=flux.at[gz, row_from], dst_ref=flux.at[gz, row_to],
                    send_sem=flux_ssem.at[kind, z], recv_sem=flux_rsem.at[kind, gz],
                    device_id=peer, device_id_type=MESH,
                ),
                landed=pltpu.make_async_remote_copy(
                    src_ref=flux.at[z, row_to], dst_ref=flux.at[z, row_to],
                    send_sem=flux_ssem.at[kind, z], recv_sem=flux_rsem.at[kind, z],
                    device_id=peer, device_id_type=MESH,
                ),
            ))

    pl.semaphore_wait(barrier, count)
    order = sorted(range(len(messages)), key=lambda n: (messages[n]["kind"][0] is None, abs(messages[n]["kind"][1]) + abs(messages[n]["kind"][2])))
    for n in order:
        guard(messages[n]["sends"], messages[n]["copy"].start)
    for entry in wall:
        guard(entry["sends"], entry["copy"].start)
    for where in along("gy"):
        pl.semaphore_signal(known_a, inc=1, device_id={"gy": where}, device_id_type=MESH)

    loads[5].wait()
    loads[6].wait()
    cond_max, cap_max, cap_min = cond_tab[0], cap_tab[0], cap_tab[0]
    for m in range(1, 8):
        cond_max = jnp.maximum(cond_max, cond_tab[m])
        cap_max = jnp.maximum(cap_max, cap_tab[m])
        cap_min = jnp.minimum(cap_min, cap_tab[m])
    highest = cap_max + 12.0 * cond_max
    center = 0.5 * (highest + cap_min)
    half_width = jnp.full((8, 128), 0.5 * (highest - cap_min), jnp.float32)
    scale = 2.0 / half_width

    def lookup(material, table):
        value = jnp.zeros_like(material)
        for m in range(8):
            value = jnp.where(material == m, table[m], value)
        return value

    def tall(tile, rows):
        return jnp.concatenate([tile] * (rows // 8), axis=0)

    lane40 = tall(lane, 40)
    inner40 = tall(inner, 40)
    group40 = tall(group, 40)
    scale40 = tall(scale, 40)

    for n in order:
        guard(messages[n]["takes"], messages[n]["landed"].wait_recv)
    if ny > 1:
        pl.semaphore_wait(known_a, ny - 1)
    for where in along("gx"):
        pl.semaphore_signal(known_b, inc=1, device_id={"gx": where}, device_id_type=MESH)

    for k in range(6):
        corners = [
            jnp.where(inner < 4, corner_in[x_index, 1, k], corner_in[x_index, 0, k])
            for x_index in range(len(sides))
        ]
        for f in range(3):
            tile = jnp.where(inner < 4, strip_in[1, f, k], strip_in[0, f, k])
            for side, beside in zip(sides, corners):
                moved = pltpu.roll(beside, lax.rem(8 * side["ghost"] - 32 * f + 128, 128), axis=1)
                hit = jnp.logical_and(group >= side["ghost"], group < side["ghost"] + 4)
                tile = jnp.where(hit, moved, tile)
            strip[f, 8 * k:8 * k + 8, :] = tile

    for i in range(slots):
        condm[i + 1] = lookup(fields[MAT, i + 1], cond_tab)
    conds[...] = lookup(strip[MAT], cond_tab)
    cond_strip = conds[4:44, :]
    beside = jnp.zeros((40, 128), jnp.float32)
    scale48 = tall(scale, 48)
    for i in range(slots):
        here = condm[i + 1, 4:44, :]
        beside = jnp.where(group40 == i, pltpu.roll(here, 8 * i + 4, axis=1), beside)
        edge = pltpu.roll(cond_strip, 124 - 8 * i, axis=1)
        low = harmonic(jnp.where(lane40 == 0, edge, pltpu.roll(here, 1, axis=1)), here) * scale40
        high = harmonic(jnp.where(lane40 == 127, edge, pltpu.roll(here, 127, axis=1)), here) * scale40
        kzl[i] = low
        kzh[i] = high
        kx[i] = harmonic(condm[i, 4:44, :], here) * scale40
        if i == slots - 1:
            kx[slots] = harmonic(condm[slots + 1, 4:44, :], here) * scale40
        ky[i, 4:44, :] = harmonic(condm[i + 1, 3:43, :], here) * scale40
        ky[i, 40:48, :] = harmonic(condm[i + 1, 39:47, :], condm[i + 1, 40:48, :]) * scale
    for i in range(slots):
        cap = lookup(fields[MAT, i + 1, 4:44, :], cap_tab)
        diag[i] = (
            (cap - center) * scale40 + kx[i] + kx[i + 1] + ky[i, 4:44, :] + ky[i, 5:45, :] + kzl[i] + kzh[i]
        )
    nothing = jnp.zeros((40, 128), jnp.float32)
    sk[0] = jnp.where(jnp.logical_or(inner40 == 0, inner40 == 4), nothing, harmonic(pltpu.roll(cond_strip, 1, axis=1), cond_strip) * scale40)
    sk[1] = jnp.where(jnp.logical_or(inner40 == 3, inner40 == 7), nothing, harmonic(pltpu.roll(cond_strip, 127, axis=1), cond_strip) * scale40)
    sk[2] = harmonic(pltpu.roll(cond_strip, 8, axis=1), cond_strip) * scale40
    sk[3] = harmonic(pltpu.roll(cond_strip, 120, axis=1), cond_strip) * scale40
    sk[4] = jnp.where(jnp.logical_or(inner40 == 3, inner40 == 4), harmonic(beside, cond_strip) * scale40, nothing)
    sy[4:44, :] = harmonic(conds[3:43, :], cond_strip) * scale40
    sy[40:48, :] = harmonic(conds[39:47, :], conds[40:48, :]) * scale
    sdiag[...] = (
        (lookup(strip[MAT, 4:44, :], cap_tab) - center) * scale40
        + sk[0] + sk[1] + sk[2] + sk[3] + sk[4] + sy[4:44, :] + sy[5:45, :]
    )

    def sweep(source, before, target, start, length, last):
        row, tall_by = (8, 32) if last else (4, 40)
        edges = strip[source, row:row + tall_by, :]
        if not isinstance(start, int):
            edges = pltpu.roll(edges, lax.rem(128 - 8 * start, 128), axis=1)
        c = slice(row - 4, row - 4 + tall_by)
        lanes = tall(lane, tall_by)
        for i in range(length):
            at = start + i
            v = fields[source, at + 1, row:row + tall_by, :]
            edge = pltpu.roll(edges, 124 - 8 * i, axis=1)
            zl = jnp.where(lanes == 0, edge, pltpu.roll(v, 1, axis=1))
            zh = jnp.where(lanes == 127, edge, pltpu.roll(v, 127, axis=1))
            acc = diag[at, c, :] * v
            acc = acc - kx[at, c, :] * fields[source, at, row:row + tall_by, :]
            acc = acc - kx[at + 1, c, :] * fields[source, at + 2, row:row + tall_by, :]
            acc = acc - ky[at, row:row + tall_by, :] * fields[source, at + 1, row - 1:row - 1 + tall_by, :]
            acc = acc - ky[at, row + 1:row + 1 + tall_by, :] * fields[source, at + 1, row + 1:row + 1 + tall_by, :]
            acc = acc - kzl[at, c, :] * zl - kzh[at, c, :] * zh
            if before is None:
                acc = 0.5 * acc
            else:
                acc = acc - fields[before, at + 1, row:row + tall_by, :]
            fields[target, at + 1, row:row + tall_by, :] = acc
        if last:
            return
        beside = jnp.zeros((40, 128), jnp.float32)
        for i in range(slots):
            beside = jnp.where(group40 == i, pltpu.roll(fields[source, i + 1, 4:44, :], 8 * i + 4, axis=1), beside)
        v = edges if isinstance(start, int) else strip[source, 4:44, :]
        acc = sdiag[...] * v - sk[4] * beside
        for n, amount in enumerate((1, 127, 8, 120)):
            acc = acc - sk[n] * pltpu.roll(v, amount, axis=1)
        acc = acc - sy[4:44, :] * strip[source, 3:43, :] - sy[5:45, :] * strip[source, 5:45, :]
        if before is None:
            acc = 0.5 * acc
        else:
            acc = acc - strip[before, 4:44, :]
        strip[target, 4:44, :] = acc

    def chain(terms, degree):
        for t in range(1, degree + 1):
            shrink = STEPS - degree + t
            if nx == 2:
                start, length = shrink * gx, 12 - shrink
            else:
                start, length = shrink, 16 - 2 * shrink
            if t == degree:
                start, length = own, 8
            sweep(terms[t - 1], terms[t - 2] if t > 1 else None, terms[t], start, length, t == degree)

    def term(i):
        return fields[TERMS[i], pl.ds(own1, 8), pl.ds(8, 32), :].reshape(32, 8, 128)

    def gram_part(total, pairs):
        for i, j in pairs:
            product = term(i) * term(j)
            value = tree([tree([product[8 * a + g] for a in range(4)]) for g in range(8)])
            value = jnp.sum(value, axis=1, keepdims=True) if False else value
            value = jnp.sum(value, axis=1, keepdims=True)
            total = jnp.where(lane == SLOT[(i, j)], value, total)
        return total

    for entry in wall:
        guard(entry["takes"], entry["landed"].wait_recv)
    for n in order:
        guard(messages[n]["sends"], messages[n]["copy"].wait_send)

    def find(k, wanted):
        holder, index = wanted // 128, lax.rem(wanted, 128)
        value = jnp.zeros((8, 128), jnp.float32)
        for q in range(nz):
            found = jnp.take_along_axis(flux[q, 8 * k:8 * k + 8, :], index, axis=1)
            value = jnp.where(holder == q, found, value)
        return value

    def add_wall():
        for k in range(6):
            rows = slice(8 * k, 8 * k + 8)
            fields[S0, own1 + 7, rows, :] = fields[S0, own1 + 7, rows, :] + find(k, map_ref[rows, :])
            wanted = jnp.where(inner < 4, strip_in[1, 3, k], strip_in[0, 3, k]).astype(jnp.int32)
            strip[S0, rows, :] = strip[S0, rows, :] + jnp.where(group == own + 7, find(k, wanted), 0.0)

    pl.when(is_top)(add_wall)

    chain(TERMS[:STEPS + 1], STEPS)
    total = gram_part(jnp.zeros((8, 128), jnp.float32), [(i, j) for i, j in PAIRS if j <= STEPS])
    chain(TERMS[STEPS + 1:], STEPS - 1)
    total = gram_part(total, [(i, j) for i, j in PAIRS if j > STEPS])
    if nx > 1:
        pl.semaphore_wait(known_b, nx - 1)

    def peers(axes):
        found = [{}]
        for axis in axes:
            found = [dict(entry, **{axis: o}) for entry in found for o in range(sizes[axis])]
        found = [entry for entry in found if any(entry.values())]
        return [
            {axis: lax.rem(pos[axis] + o, sizes[axis]) for axis, o in entry.items()} for entry in found
        ]

    def index_of(axes, where):
        index = 0
        for axis in axes:
            index = index * sizes[axis] + where[axis]
        return index

    row = jnp.sum(total, axis=0, keepdims=True)
    base = 0
    gram_copies = []
    for stage, axes in enumerate(stages):
        members = 1
        for axis in axes:
            members *= sizes[axis]
        mine = base + index_of(axes, pos)
        gram_send[stage] = row
        gram_halo[mine] = row
        for peer in peers(axes):
            other = base + index_of(axes, peer)
            copy = pltpu.make_async_remote_copy(
                src_ref=gram_send.at[stage], dst_ref=gram_halo.at[mine],
                send_sem=gram_ssem.at[other], recv_sem=gram_rsem.at[mine],
                device_id=peer, device_id_type=MESH,
            )
            copy.start()
            gram_copies.append(copy)
        for peer in peers(axes):
            other = base + index_of(axes, peer)
            pltpu.make_async_remote_copy(
                src_ref=gram_halo.at[other], dst_ref=gram_halo.at[other],
                send_sem=gram_ssem.at[other], recv_sem=gram_rsem.at[other],
                device_id=peer, device_id_type=MESH,
            ).wait_recv()
        row = tree([gram_halo[base + member] for member in range(members)])
        base += members

    gram = [[None] * DIM for _ in range(DIM)]
    for (i, j), k in SLOT.items():
        gram[i][j] = gram[j][i] = jnp.broadcast_to(row[:, k:k + 1], (8, 128))
    moved, residue, direct = coefficients(gram, jnp.full((8, 128), center, jnp.float32), half_width)

    stores = []
    loads[7].wait()
    for number, weights, out in ((1, residue, res_out), (2, direct, dir_out), (0, moved, sol_out)):
        summed = held[0].reshape(32, 8, 128) if number == 0 else None
        for i in range(DIM):
            if weights[i] is not None:
                summed = plus(summed, weights[i][None] * term(i))
        held[number] = summed.reshape(8, 32, 128)
        stores.append(pltpu.make_async_copy(held.at[number], out, store_sem.at[number]))
        stores[-1].start()

    for entry in wall:
        guard(entry["sends"], entry["copy"].wait_send)
    for copy in gram_copies:
        copy.wait_send()
    for store in stores:
        store.wait()


def finish(res_in, dir_in, sol_in, res_out, dir_out, sol_out, held, load_sem, store_sem):
    loads = []
    for source in (res_in, dir_in, sol_in):
        k = len(loads)
        loads.append(pltpu.make_async_copy(source, held.at[k], load_sem.at[k]))
        loads[k].start()
    stores = []
    for target in (res_out, dir_out, sol_out):
        k = len(stores)
        loads[k].wait()
        stores.append(pltpu.make_async_copy(held.at[k], target, store_sem.at[k]))
        stores[k].start()
    for store in stores:
        store.wait()


def solution(mesh):
    sizes = {axis: mesh.shape[axis] for axis in AXES}
    total = sizes["gx"] * sizes["gy"] * sizes["gz"]
    stages = [AXES] if total <= 64 else [(axis,) for axis in AXES]
    rows = 0
    for axes in stages:
        members = 1
        for axis in axes:
            members *= sizes[axis]
        rows += members
    slots = 12 if sizes["gx"] == 2 else 16
    sides = 1 if sizes["gx"] == 2 else 2
    parts = message_count(sizes)
    nz = sizes["gz"]

    def body(sol, res, direction, material, cond_table, cap_table, gas, supply):
        hbm = pl.BlockSpec(memory_space=pltpu.HBM)
        f32 = jnp.float32
        block = jax.ShapeDtypeStruct((8, 32, 128), f32)
        dma = pltpu.SemaphoreType.DMA
        fields = pl.pallas_call(
            lambda *refs: kernel(sizes, stages, *refs),
            out_shape=(block, block, block),
            in_specs=[hbm] * 8,
            out_specs=(hbm, hbm, hbm),
            scratch_shapes=[
                pltpu.VMEM((FIELDS, slots + 2, 48, 128), f32),
                pltpu.VMEM((FIELDS, 48, 128), f32),
                pltpu.VMEM((3, 8, 32, 128), f32),
                pltpu.SMEM((8,), f32),
                pltpu.SMEM((8,), f32),
                pltpu.VMEM((8, 32, 128), jnp.int32),
                pltpu.VMEM((nz, 48, 128), f32),
                pltpu.VMEM((48, 128), jnp.int32),
                pltpu.VMEM((slots + 2, 48, 128), f32),
                pltpu.VMEM((slots, 40, 128), f32),
                pltpu.VMEM((slots + 1, 40, 128), f32),
                pltpu.VMEM((slots, 48, 128), f32),
                pltpu.VMEM((slots, 40, 128), f32),
                pltpu.VMEM((slots, 40, 128), f32),
                pltpu.VMEM((48, 128), f32),
                pltpu.VMEM((40, 128), f32),
                pltpu.VMEM((5, 40, 128), f32),
                pltpu.VMEM((48, 128), f32),
                pltpu.VMEM((4, 4, 8, 128), f32),
                pltpu.VMEM((sides, 4, 8, 128), f32),
                pltpu.VMEM((2, 4, 6, 8, 128), f32),
                pltpu.VMEM((sides, 2, 6, 8, 128), f32),
                pltpu.VMEM((len(stages), 1, 128), f32),
                pltpu.VMEM((rows, 1, 128), f32),
                dma((parts,)),
                dma((parts,)),
                dma((3, nz)),
                dma((3, nz)),
                dma((2,)),
                dma((2,)),
                dma((rows,)),
                dma((rows,)),
                dma((8,)),
                dma((3,)),
                pltpu.SemaphoreType.REGULAR,
                pltpu.SemaphoreType.REGULAR,
            ],
            compiler_params=pltpu.CompilerParams(
                collective_id=0, has_side_effects=True, vmem_limit_bytes=VMEM
            ),
            cost_estimate=pl.CostEstimate(flops=10**7, bytes_accessed=10**6, transcendentals=0),
        )(cond_table, cap_table, sol, res, direction, material, gas, supply)
        outs = pl.pallas_call(
            finish,
            out_shape=(block, block, block),
            in_specs=[hbm] * 3,
            out_specs=(hbm, hbm, hbm),
            scratch_shapes=[
                pltpu.VMEM((3, 8, 32, 128), f32),
                pltpu.SemaphoreType.DMA((3,)),
                pltpu.SemaphoreType.DMA((3,)),
            ],
            compiler_params=pltpu.CompilerParams(vmem_limit_bytes=VMEM),
        )(fields[1], fields[2], fields[0])
        return outs[2], outs[0], outs[1]

    spec = P("gx", "gy", "gz")
    in_specs = (spec, spec, spec, spec, P(), P(), P("gy", "gz"), P("gy", "gz"))
    return jax.shard_map(
        body, mesh=mesh, in_specs=in_specs, out_specs=(spec, spec, spec), check_vma=False
    )
```

```python
import jax
import jax.numpy as jnp
from jax import lax
from jax.experimental import pallas as pl
from jax.experimental.pallas import tpu as pltpu
from jax.sharding import PartitionSpec as P

STEPS = 4
VMEM = 64 * 1024 * 1024
AXES = ("gx", "gy", "gz")
MESH = pl.DeviceIdType.MESH
DIM = 2 * STEPS + 1
PAIRS = [(i, j) for i in range(DIM) for j in range(i, DIM)]
SLOT = {pair: k for k, pair in enumerate(PAIRS)}


def harmonic(a, b):
    return 2.0 * a * b / jnp.maximum(a + b, 1e-30)


def tree(parts):
    while len(parts) > 1:
        parts = [sum(parts[k:k + 2][1:], parts[k]) for k in range(0, len(parts), 2)]
    return parts[0]


def times(a, b):
    return None if a is None or b is None else a * b


def plus(a, b):
    return b if a is None else a if b is None else a + b


def shift_product(p, center, half_width):
    q = [None] * DIM
    for offset, length in ((0, STEPS + 1), (STEPS + 1, STEPS)):
        for column in range(length - 1):
            entry = p[offset + column]
            if entry is None:
                continue
            q[offset + column] = plus(q[offset + column], center * entry)
            low = half_width if column == 0 else 0.5 * half_width
            q[offset + column + 1] = plus(q[offset + column + 1], low * entry)
            if column >= 1:
                q[offset + column - 1] = plus(q[offset + column - 1], 0.5 * half_width * entry)
    return q


def form(gram, a, b):
    total = None
    for i in range(DIM):
        if a[i] is None:
            continue
        row = None
        for j in range(DIM):
            row = plus(row, times(gram[i][j], b[j]))
        total = plus(total, a[i] * row)
    return total


def coefficients(gram, center, half_width):
    one = jnp.ones_like(gram[0][0])
    p = [None] * DIM
    r = [None] * DIM
    x = [None] * DIM
    p[0] = one
    r[STEPS + 1] = one
    rr = form(gram, r, r)
    for _ in range(STEPS):
        q = shift_product(p, center, half_width)
        step = rr / form(gram, p, q)
        x = [plus(x[i], times(step, p[i])) for i in range(DIM)]
        r = [plus(r[i], times(-step, q[i])) for i in range(DIM)]
        new = form(gram, r, r)
        ratio = new / rr
        p = [plus(r[i], times(ratio, p[i])) for i in range(DIM)]
        rr = new
    return x, r, p


MAT, D0, S0 = 0, 1, 2
TERMS = [D0, 3, 4, 5, 6, S0, 7, 8, 9]
FIELDS = 10


EDGE = []
for _field, _depth in ((MAT, 4), (D0, 4), (S0, 3)):
    for _i in range(1, _depth):
        EDGE.append((_field, _i, _depth - _i, sum(entry[2] for entry in EDGE)))


def both(*conditions):
    kept = [c for c in conditions if c is not True]
    if not kept:
        return True
    total = kept[0]
    for c in kept[1:]:
        total = jnp.logical_and(total, c)
    return total


def guard(condition, action):
    if condition is True:
        action()
    else:
        pl.when(condition)(action)


def layout(gx, count):
    if count == 2:
        own = 4 * gx
        sides = [dict(
            peer=1 - gx, send=True, recv=True, ghost=8 * (1 - gx),
            src4=4, dst4=8 * gx, in4=8 * (1 - gx),
            src3=5 - gx, dst3=1 + 7 * gx, in3=1 + 7 * (1 - gx),
            first=4 * (1 - gx), face=8 - 4 * gx, beside=7 - 3 * gx,
            near=lambda i: 8 - i + gx * (2 * i - 5), far=lambda i: 7 + i - gx * (2 * i + 3),
        )]
        return 12, own, sides
    own = 4
    sides = [
        dict(peer=gx - 1, send=gx > 0, recv=gx < count - 1, ghost=12,
             src4=4, dst4=12, in4=12, src3=4, dst3=12, in3=12, first=0, face=12, beside=11,
             near=lambda i: 3 + i, far=lambda i: 11 + i),
        dict(peer=gx + 1, send=gx < count - 1, recv=gx > 0, ghost=0,
             src4=8, dst4=0, in4=0, src3=9, dst3=1, in3=1, first=4, face=4, beside=4,
             near=lambda i: 12 - i, far=lambda i: 4 - i),
    ]
    return 16, own, sides


def message_count(sizes):
    sides = 1 if sizes["gx"] == 2 else 2
    return 8 + sides * 10


def kernel(
    sizes, stages, cond_in, cap_in, sol_in, res_in, dir_in, mat_in, gas_in, map_in,
    fields, tail, sol_ref,
    strip, cond_tab, cap_tab, mat_ref, flux, map_ref,
    condm, diag, kx, ky, kzl, kzh, conds, sdiag, sk, sy, aside,
    pack, corner, edge, strip_in, corner_in, edge_in, gram_send, gram_halo,
    send_sem, recv_sem, flux_ssem, flux_rsem, map_ssem, map_rsem,
    gram_ssem, gram_rsem, load_sem, known,
):
    pos = {axis: lax.axis_index(axis) for axis in AXES}
    gx, gy, gz = (pos[axis] for axis in AXES)
    nx, ny, nz = (sizes[axis] for axis in AXES)
    slots, own, sides = layout(gx, nx)
    is_top = gx == nx - 1
    lane = lax.broadcasted_iota(jnp.int32, (8, 128), 1)
    group = lane // 8
    inner = lax.rem(lane, 8)
    own1 = own + 1

    loads = []
    for source, target in (
        (mat_in, mat_ref),
        (dir_in, fields.at[D0, pl.ds(own1, 8), pl.ds(8, 32)]),
        (res_in, fields.at[S0, pl.ds(own1, 8), pl.ds(8, 32)]),
        (map_in, map_ref.at[pl.ds(8, 32)]),
        (gas_in, flux.at[gz, pl.ds(8, 32)]),
        (cond_in, cond_tab), (cap_in, cap_tab),
        (sol_in, sol_ref),
    ):
        loads.append(pltpu.make_async_copy(source, target, load_sem.at[len(loads)]))
        loads[-1].start()

    barrier = pltpu.get_barrier_semaphore()
    count = jnp.int32(0)

    def inside(axis, step):
        if step == 0:
            return True
        return pos[axis] > 0 if step < 0 else pos[axis] < sizes[axis] - 1

    def greet(condition, peer):
        nonlocal count
        guard(condition, lambda: pl.semaphore_signal(barrier, inc=1, device_id=peer, device_id_type=MESH))
        count = count + (1 if condition is True else jnp.where(condition, 1, 0))

    def along(axis):
        return [lax.rem(pos[axis] + o, sizes[axis]) for o in range(1, sizes[axis])]

    for side in [None] + sides:
        for dy in (-1, 0, 1):
            for dz in (-1, 0, 1):
                if side is None and not dy and not dz:
                    continue
                peer = {"gy": gy + dy, "gz": gz + dz}
                if side is not None:
                    peer["gx"] = side["peer"]
                greet(
                    both(True if side is None else side["send"], inside("gy", dy), inside("gz", dz)), peer
                )

    def spread(number, axis):
        n, p = sizes[axis], pos[axis]
        for s in range(n - 2):
            for way, step in ((0, -1), (1, 1)):
                here = jnp.logical_and(p >= 1, p + 1 + s <= n - 1) if way == 0 else jnp.logical_and(p <= n - 2, p - 1 - s >= 0)
                guard(here, lambda: pl.semaphore_signal(
                    known.at[2 * number + way], inc=1, device_id={axis: p + step}, device_id_type=MESH))
            for way, there in ((0, p + 2 + s <= n - 1), (1, p - 2 - s >= 0)):
                guard(there, lambda: pl.semaphore_wait(known.at[2 * number + way], 1))

    def blank(condition, slot_start, slot_count, rows):
        def fill():
            for f, value in ((MAT, -1.0), (D0, 0.0), (S0, 0.0)):
                fields[f, pl.ds(slot_start, slot_count), rows, :] = jnp.full(
                    (slot_count, rows.stop - rows.start, 128), value, jnp.float32
                )
        guard(condition, fill)

    low_rows, high_rows = slice(0, 8), slice(40, 48)
    blank(gy == 0, 1, slots, low_rows)
    blank(gy == ny - 1, 1, slots, high_rows)
    for side in sides:
        if side["recv"] is not True:
            blank(jnp.logical_not(side["recv"]), side["in4"] + 1, 4, slice(0, 48))
    zeros48 = jnp.zeros((48, 128), jnp.float32)
    for f in range(FIELDS):
        fields[f, 0] = zeros48
        fields[f, slots + 1] = zeros48
    condm[0] = zeros48
    condm[slots + 1] = zeros48

    def blank_strip(condition, dz_index, rows):
        def fill():
            for k in rows:
                strip_in[dz_index, k] = jnp.where(lane < 32, -1.0, 0.0)
        guard(condition, fill)

    def blank_corner(condition, x_index, dz_index, rows):
        def fill():
            for k in rows:
                corner_in[x_index, dz_index, k] = jnp.where(lane < 16, -1.0, 0.0)
        guard(condition, fill)

    for dz_index, alone in ((0, gz == 0), (1, gz == nz - 1)):
        blank_strip(alone, dz_index, range(6))
        blank_strip(gy == 0, dz_index, [0])
        blank_strip(gy == ny - 1, dz_index, [5])
        for x_index, side in enumerate(sides):
            blank_corner(alone, x_index, dz_index, range(6))
            blank_corner(gy == 0, x_index, dz_index, [0])
            blank_corner(gy == ny - 1, x_index, dz_index, [5])
            if side["recv"] is not True:
                blank_corner(jnp.logical_not(side["recv"]), x_index, dz_index, range(6))

    def blank_flux(condition, rows):
        def fill():
            flux[:, rows, :] = jnp.zeros((nz, 8, 128), jnp.float32)
            map_ref[rows, :] = jnp.zeros((8, 128), jnp.int32)
        guard(condition, fill)

    blank_flux(gy == 0, low_rows)
    blank_flux(gy == ny - 1, high_rows)

    messages = []
    for x_index, side in [(None, None)] + list(enumerate(sides)):
        for dy in (-1, 0, 1):
            for dz in (-1, 0, 1):
                if side is None and not dy and not dz:
                    continue
                sends = both(inside("gy", dy), inside("gz", dz))
                takes = both(inside("gy", -dy), inside("gz", -dz))
                peer = {}
                if dy:
                    peer["gy"] = gy + dy
                if dz:
                    peer["gz"] = gz + dz
                if side is not None:
                    sends = both(sends, side["send"])
                    takes = both(takes, side["recv"])
                    peer["gx"] = side["peer"]
                row_from = pl.ds(8, 32) if not dy else pl.ds(32, 8) if dy > 0 else pl.ds(8, 8)
                row_to = pl.ds(8, 32) if not dy else pl.ds(0, 8) if dy > 0 else pl.ds(40, 8)
                tile_from = pl.ds(0, 4) if not dy else pl.ds(3, 1) if dy > 0 else pl.ds(0, 1)
                tile_to = pl.ds(1, 4) if not dy else pl.ds(0, 1) if dy > 0 else pl.ds(5, 1)
                came = 0 if dz > 0 else 1
                if side is None and not dz:
                    parts = [(
                        fields.at[pl.ds(0, 3), pl.ds(own1, 8), row_from],
                        fields.at[pl.ds(0, 3), pl.ds(own1, 8), row_to],
                        fields.at[pl.ds(0, 3), pl.ds(own1, 8), row_to],
                    )]
                elif side is None:
                    target = strip_in.at[came, tile_to]
                    parts = [(pack.at[came, tile_from], target, target)]
                elif dz:
                    target = corner_in.at[x_index, came, tile_to]
                    parts = [(corner.at[x_index, came, tile_from], target, target)]
                elif dy:
                    target = edge_in.at[x_index, (dy + 1) // 2]
                    parts = [(edge.at[x_index, (dy + 1) // 2], target, target)]
                else:
                    parts = [tuple(
                        fields.at[pl.ds(0, 2), pl.ds(side[name] + 1, 4), row_from]
                        for name in ("src4", "dst4", "in4")
                    ), tuple(
                        fields.at[S0, pl.ds(side[name] + 1, 3), row_from]
                        for name in ("src3", "dst3", "in3")
                    )]
                for source, target, landing in parts:
                    number = len(messages)
                    messages.append(dict(
                        sends=sends, takes=takes, kind=(x_index, dy, dz),
                        copy=pltpu.make_async_remote_copy(
                            src_ref=source, dst_ref=target,
                            send_sem=send_sem.at[number], recv_sem=recv_sem.at[number],
                            device_id=peer, device_id_type=MESH,
                        ),
                        landed=pltpu.make_async_remote_copy(
                            src_ref=landing, dst_ref=landing,
                            send_sem=send_sem.at[number], recv_sem=recv_sem.at[number],
                            device_id=peer, device_id_type=MESH,
                        ),
                    ))

    wall = []
    for kind, dy in enumerate((0, -1, 1)):
        row_from = pl.ds(8, 32) if not dy else pl.ds(32, 8) if dy > 0 else pl.ds(8, 8)
        row_to = pl.ds(8, 32) if not dy else pl.ds(0, 8) if dy > 0 else pl.ds(40, 8)
        sends = both(is_top, inside("gy", dy))
        takes = both(is_top, inside("gy", -dy))
        if dy:
            wall.append(dict(
                sends=sends, takes=takes,
                copy=pltpu.make_async_remote_copy(
                    src_ref=map_ref.at[row_from], dst_ref=map_ref.at[row_to],
                    send_sem=map_ssem.at[kind - 1], recv_sem=map_rsem.at[kind - 1],
                    device_id={"gy": gy + dy}, device_id_type=MESH,
                ),
                landed=pltpu.make_async_remote_copy(
                    src_ref=map_ref.at[row_to], dst_ref=map_ref.at[row_to],
                    send_sem=map_ssem.at[kind - 1], recv_sem=map_rsem.at[kind - 1],
                    device_id={"gy": gy - dy}, device_id_type=MESH,
                ),
            ))
        for o in range(nz):
            if not dy and not o:
                continue
            z = lax.rem(gz + o, nz)
            peer = {"gy": gy + dy, "gz": z}
            wall.append(dict(
                sends=sends, takes=takes,
                copy=pltpu.make_async_remote_copy(
                    src_ref=flux.at[gz, row_from], dst_ref=flux.at[gz, row_to],
                    send_sem=flux_ssem.at[kind, z], recv_sem=flux_rsem.at[kind, gz],
                    device_id=peer, device_id_type=MESH,
                ),
                landed=pltpu.make_async_remote_copy(
                    src_ref=flux.at[z, row_to], dst_ref=flux.at[z, row_to],
                    send_sem=flux_ssem.at[kind, z], recv_sem=flux_rsem.at[kind, z],
                    device_id=peer, device_id_type=MESH,
                ),
            ))

    def start(test):
        for entry in messages:
            if test(*entry["kind"]):
                guard(entry["sends"], entry["copy"].start)

    def finish(test):
        for entry in messages:
            if test(*entry["kind"]):
                guard(entry["takes"], entry["landed"].wait_recv)

    loads[0].wait()
    fields[MAT, pl.ds(own1, 8), pl.ds(8, 32), :] = mat_ref[...].astype(jnp.float32)
    loads[1].wait()
    loads[2].wait()
    pl.semaphore_wait(barrier, count)
    start(lambda x, y, z: x is not None and not y and not z)
    start(lambda x, y, z: x is None and y and not z)

    for x_index, side in enumerate(sides):
        for which in range(2):
            for f, i, n, offset in EDGE:
                first = 40 - n if which else 8
                edge[x_index, which, offset:offset + n, :] = fields[f, side["near"](i) + 1, first:first + n, :]
    start(lambda x, y, z: x is not None and y and not z)

    loads[3].wait()
    for k in range(4):
        rows = slice(8 + 8 * k, 16 + 8 * k)
        wide = []
        for f in range(3):
            tile = jnp.zeros((8, 128), jnp.float32)
            for i in range(8):
                moved = pltpu.roll(fields[f, own1 + i, rows, :], 8 * i + 4, axis=1)
                tile = jnp.where(group == i, moved, tile)
            wide.append(tile)
        wide.append(pltpu.roll(map_ref[rows, :].astype(jnp.float32), 8 * 7 + 4, axis=1))
        for came in range(2):
            tile = jnp.zeros((8, 128), jnp.float32)
            source = 8 * (lax.rem(lane, 32) // 4) + lax.rem(lane, 4) + 4 * came
            for f in range(4):
                tile = jnp.where(lane // 32 == f, jnp.take_along_axis(wide[f], source, axis=1), tile)
            pack[came, k] = tile
            for x_index, side in enumerate(sides):
                tile = jnp.zeros((8, 128), jnp.float32)
                source = 8 * (lax.rem(lane, 16) // 4 + side["first"]) + lax.rem(lane, 4) + 4 * came
                for f in range(3):
                    tile = jnp.where(lane // 16 == f, jnp.take_along_axis(wide[f], source, axis=1), tile)
                corner[x_index, came, k] = tile
    start(lambda x, y, z: z)
    loads[4].wait()
    spread(0, "gz")
    for entry in wall:
        guard(entry["sends"], entry["copy"].start)

    loads[5].wait()
    loads[6].wait()
    cond_max, cap_max, cap_min = cond_tab[0], cap_tab[0], cap_tab[0]
    for m in range(1, 8):
        cond_max = jnp.maximum(cond_max, cond_tab[m])
        cap_max = jnp.maximum(cap_max, cap_tab[m])
        cap_min = jnp.minimum(cap_min, cap_tab[m])
    highest = cap_max + 12.0 * cond_max
    center = 0.5 * (highest + cap_min)
    half_width = jnp.full((8, 128), 0.5 * (highest - cap_min), jnp.float32)
    scale = 2.0 / half_width

    def lookup(material, table):
        value = jnp.zeros_like(material)
        for m in range(8):
            value = jnp.where(material == m, table[m], value)
        return value

    def tall(tile, rows):
        return jnp.concatenate([tile] * (rows // 8), axis=0)

    lane40 = tall(lane, 40)
    inner40 = tall(inner, 40)
    group40 = tall(group, 40)
    scale40 = tall(scale, 40)

    def span(first, value, otherwise, count):
        return jnp.where(jnp.logical_and(group >= first, group < first + count), value, otherwise)

    def join(k, f):
        source = 32 * f + 4 * jnp.clip(group - own, 0, 7) + 3 - lax.rem(inner, 4)
        high = jnp.take_along_axis(strip_in[1, k], source, axis=1)
        low = jnp.take_along_axis(strip_in[0, k], source, axis=1)
        return jnp.where(inner < 4, high, low)

    def join_corner(k, f, x_index):
        source = 16 * f + 4 * jnp.clip(group - sides[x_index]["ghost"], 0, 3) + 3 - lax.rem(inner, 4)
        high = jnp.take_along_axis(corner_in[x_index, 1, k], source, axis=1)
        low = jnp.take_along_axis(corner_in[x_index, 0, k], source, axis=1)
        return jnp.where(inner < 4, high, low)

    scale48 = tall(scale, 48)
    nothing = jnp.zeros((40, 128), jnp.float32)

    def collect(value_of, first, count):
        tile = nothing
        for i in range(count):
            tile = jnp.where(group40 == i, pltpu.roll(value_of(first + i), 8 * i + 4, axis=1), tile)
        if isinstance(first, int):
            return pltpu.roll(tile, 8 * first, axis=1) if first else tile
        return pltpu.roll(tile, lax.rem(8 * first, 128), axis=1)

    def strip_edges(source, first):
        tile = strip_cond() if source is None else strip[source, 4:44, :]
        if isinstance(first, int):
            return pltpu.roll(tile, (128 - 8 * first) % 128, axis=1) if first else tile
        return pltpu.roll(tile, lax.rem(128 - 8 * first, 128), axis=1)

    def strip_cond():
        return conds[4:44, :]

    def main_coefficients(first, count):
        edges = strip_edges(None, first)
        for i in range(count):
            at = first + i
            here = condm[at + 1, 4:44, :]
            edge_value = pltpu.roll(edges, 124 - 8 * i, axis=1)
            low = harmonic(jnp.where(lane40 == 0, edge_value, pltpu.roll(here, 1, axis=1)), here) * scale40
            high = harmonic(jnp.where(lane40 == 127, edge_value, pltpu.roll(here, 127, axis=1)), here) * scale40
            kzl[at] = low
            kzh[at] = high
            ky[at, 4:44, :] = harmonic(condm[at + 1, 3:43, :], here) * scale40
            ky[at, 40:48, :] = harmonic(condm[at + 1, 39:47, :], condm[at + 1, 40:48, :]) * scale
            cap = lookup(fields[MAT, at + 1, 4:44, :], cap_tab)
            diag[at] = (
                (cap - center) * scale40 + kx[at] + kx[at + 1] + ky[at, 4:44, :] + ky[at, 5:45, :] + low + high
            )

    def strip_coefficients():
        cond_strip = strip_cond()
        sk[0] = jnp.where(jnp.logical_or(inner40 == 0, inner40 == 4), nothing, harmonic(pltpu.roll(cond_strip, 1, axis=1), cond_strip) * scale40)
        sk[1] = jnp.where(jnp.logical_or(inner40 == 3, inner40 == 7), nothing, harmonic(pltpu.roll(cond_strip, 127, axis=1), cond_strip) * scale40)
        sk[2] = harmonic(pltpu.roll(cond_strip, 8, axis=1), cond_strip) * scale40
        sk[3] = harmonic(pltpu.roll(cond_strip, 120, axis=1), cond_strip) * scale40
        sk[4] = jnp.where(jnp.logical_or(inner40 == 3, inner40 == 4), harmonic(aside[4], cond_strip) * scale40, nothing)
        sy[4:44, :] = harmonic(conds[3:43, :], cond_strip) * scale40
        sy[40:48, :] = harmonic(conds[39:47, :], conds[40:48, :]) * scale
        sdiag[...] = (
            (lookup(strip[MAT, 4:44, :], cap_tab) - center) * scale40
            + sk[0] + sk[1] + sk[2] + sk[3] + sk[4] + sy[4:44, :] + sy[5:45, :]
        )

    def sweep(source, before, target, first, count, last=False):
        row, height = (8, 32) if last else (4, 40)
        edges = strip_edges(source, first)[row - 4:row - 4 + height]
        c = slice(row - 4, row - 4 + height)
        lanes = tall(lane, height)
        for i in range(count):
            at = first + i
            v = fields[source, at + 1, row:row + height, :]
            edge_value = pltpu.roll(edges, 124 - 8 * i, axis=1)
            zl = jnp.where(lanes == 0, edge_value, pltpu.roll(v, 1, axis=1))
            zh = jnp.where(lanes == 127, edge_value, pltpu.roll(v, 127, axis=1))
            acc = diag[at, c, :] * v
            acc = acc - kx[at, c, :] * fields[source, at, row:row + height, :]
            acc = acc - kx[at + 1, c, :] * fields[source, at + 2, row:row + height, :]
            acc = acc - ky[at, row:row + height, :] * fields[source, at + 1, row - 1:row - 1 + height, :]
            acc = acc - ky[at, row + 1:row + 1 + height, :] * fields[source, at + 1, row + 1:row + 1 + height, :]
            acc = acc - kzl[at, c, :] * zl - kzh[at, c, :] * zh
            if before is None:
                acc = 0.5 * acc
            else:
                acc = acc - fields[before, at + 1, row:row + height, :]
            fields[target, at + 1, row:row + height, :] = acc

    def sweep_strip(source, before, target, boundary):
        v = strip[source, 4:44, :]
        acc = sdiag[...] * v - sk[4] * boundary
        for n, amount in enumerate((1, 127, 8, 120)):
            acc = acc - sk[n] * pltpu.roll(v, amount, axis=1)
        acc = acc - sy[4:44, :] * strip[source, 3:43, :] - sy[5:45, :] * strip[source, 5:45, :]
        if before is None:
            acc = 0.5 * acc
        else:
            acc = acc - strip[before, 4:44, :]
        strip[target, 4:44, :] = acc

    def main_of(f):
        return lambda at: fields[f, at + 1, 4:44, :]

    def chain(terms, degree):
        for t in range(1, degree + 1):
            shrink = STEPS - degree + t
            if nx == 2:
                first, count = shrink * gx, 12 - shrink
            else:
                first, count = shrink, 16 - 2 * shrink
            if t == degree:
                first, count = own, 8
            before = terms[t - 2] if t > 1 else None
            sweep(terms[t - 1], before, terms[t], first, count, t == degree)
            if t < degree:
                sweep_strip(terms[t - 1], before, terms[t], collect(main_of(terms[t - 1]), 0, slots))

    def term(i):
        return fields[TERMS[i], pl.ds(own1, 8), pl.ds(8, 32), :].reshape(32, 8, 128)

    def gram_part(total, pairs):
        for i, j in pairs:
            product = term(i) * term(j)
            value = tree([tree([product[8 * a + g] for a in range(4)]) for g in range(8)])
            value = jnp.sum(value, axis=1, keepdims=True)
            total = jnp.where(lane == SLOT[(i, j)], value, total)
        return total

    def find(k, wanted):
        holder, index = wanted // 128, lax.rem(wanted, 128)
        value = jnp.zeros((8, 128), jnp.float32)
        for q in range(nz):
            found = jnp.take_along_axis(flux[q, 8 * k:8 * k + 8, :], index, axis=1)
            value = jnp.where(holder == q, found, value)
        return value

    def add_wall():
        for k in range(6):
            rows = slice(8 * k, 8 * k + 8)
            fields[S0, own1 + 7, rows, :] = fields[S0, own1 + 7, rows, :] + find(k, map_ref[rows, :])
            wanted = join(k, 3).astype(jnp.int32)
            strip[S0, rows, :] = strip[S0, rows, :] + jnp.where(group == own + 7, find(k, wanted), 0.0)

    direction = TERMS[:STEPS + 1]
    finish(lambda x, y, z: x is None)
    for k in range(6):
        for f in range(3):
            value = join(k, f)
            strip[f, 8 * k:8 * k + 8, :] = span(own, value, -1.0, 8) if f == MAT else value
    for i in range(8):
        condm[own1 + i] = lookup(fields[MAT, own1 + i], cond_tab)
    conds[...] = lookup(strip[MAT], cond_tab)
    kx[own] = nothing
    kx[own + 8] = nothing
    for i in range(1, 8):
        kx[own + i] = harmonic(condm[own + i, 4:44, :], condm[own + i + 1, 4:44, :]) * scale40
    main_coefficients(own, 8)
    if nx == 2:
        aside[4] = collect(lambda at: condm[at + 1, 4:44, :], own, 8)
        strip_coefficients()
        for t in range(1, STEPS + 1):
            before = direction[t - 2] if t > 1 else None
            first, count = (4 + t) * gx, 8 - t
            sweep(direction[t - 1], before, direction[t], first, count, t == STEPS)
            aside[t - 1] = collect(main_of(direction[t - 1]), own, 8)
            if t < STEPS:
                sweep_strip(direction[t - 1], before, direction[t], aside[t - 1])

    finish(lambda x, y, z: x is not None)
    for x_index, side in enumerate(sides):
        for which in range(2):
            def unload():
                for f, i, n, offset in EDGE:
                    target = 8 - n if which else 40
                    fields[f, side["far"](i) + 1, target:target + n, :] = edge_in[x_index, which, offset:offset + n, :]
            guard(both(side["recv"], gy > 0 if which else gy < ny - 1), unload)
    for k in range(6):
        for x_index, side in enumerate(sides):
            for f in range(3):
                rows = slice(8 * k, 8 * k + 8)
                strip[f, rows, :] = span(side["ghost"], join_corner(k, f, x_index), strip[f, rows, :], 4)
    for side in sides:
        for g in range(4):
            condm[side["in4"] + g + 1] = lookup(fields[MAT, side["in4"] + g + 1], cond_tab)
    conds[...] = lookup(strip[MAT], cond_tab)
    aside[4] = collect(lambda at: condm[at + 1, 4:44, :], 0, slots)
    strip_coefficients()
    for side in sides:
        for g in range(5):
            at = side["in4"] + g
            kx[at] = harmonic(condm[at, 4:44, :], condm[at + 1, 4:44, :]) * scale40
        diag[side["beside"]] = diag[side["beside"]] + kx[side["face"]]
        main_coefficients(side["in4"], 4)
    if nx == 2:
        for t in range(1, STEPS + 1):
            before = direction[t - 2] if t > 1 else None
            first = 8 - t + (2 * t - 8) * gx
            sweep(direction[t - 1], before, direction[t], first, 4, t == STEPS)
            if t < STEPS:
                newer = 9 - t + (2 * t - 10) * gx
                fresh = collect(main_of(direction[t - 1]), newer, 4)
                hit = jnp.logical_and(group40 >= newer, group40 < newer + 4)
                sweep_strip(direction[t - 1], before, direction[t], jnp.where(hit, fresh, aside[t - 1]))
    else:
        chain(direction, STEPS)
    total = gram_part(jnp.zeros((8, 128), jnp.float32), [(i, j) for i, j in PAIRS if j <= STEPS])
    spread(1, "gy")
    spread(2, "gx")

    for entry in wall:
        guard(entry["takes"], entry["landed"].wait_recv)
    for entry in messages:
        guard(entry["sends"], entry["copy"].wait_send)
    pl.when(is_top)(add_wall)
    chain(TERMS[STEPS + 1:], STEPS - 1)
    total = gram_part(total, [(i, j) for i, j in PAIRS if j > STEPS])

    def peers(axes):
        found = [{}]
        for axis in axes:
            found = [dict(entry, **{axis: o}) for entry in found for o in range(sizes[axis])]
        found = [entry for entry in found if any(entry.values())]
        return [
            {axis: lax.rem(pos[axis] + o, sizes[axis]) for axis, o in entry.items()} for entry in found
        ]

    def index_of(axes, where):
        index = 0
        for axis in axes:
            index = index * sizes[axis] + where[axis]
        return index

    row = jnp.sum(total, axis=0, keepdims=True)
    base = 0
    gram_copies = []
    for stage, axes in enumerate(stages):
        members = 1
        for axis in axes:
            members *= sizes[axis]
        mine = base + index_of(axes, pos)
        gram_send[stage] = row
        gram_halo[mine] = row
        for peer in peers(axes):
            other = base + index_of(axes, peer)
            copy = pltpu.make_async_remote_copy(
                src_ref=gram_send.at[stage], dst_ref=gram_halo.at[mine],
                send_sem=gram_ssem.at[other], recv_sem=gram_rsem.at[mine],
                device_id=peer, device_id_type=MESH,
            )
            copy.start()
            gram_copies.append(copy)
        for peer in peers(axes):
            other = base + index_of(axes, peer)
            pltpu.make_async_remote_copy(
                src_ref=gram_halo.at[other], dst_ref=gram_halo.at[other],
                send_sem=gram_ssem.at[other], recv_sem=gram_rsem.at[other],
                device_id=peer, device_id_type=MESH,
            ).wait_recv()
        row = tree([gram_halo[base + member] for member in range(members)])
        base += members

    tail[0] = jnp.broadcast_to(row, (8, 128))
    tail[1] = jnp.full((8, 128), center, jnp.float32)
    tail[2] = half_width
    loads[7].wait()
    for entry in wall:
        guard(entry["sends"], entry["copy"].wait_send)
    for copy in gram_copies:
        copy.wait_send()


def combine(sizes, fields, tail, sol_ref, sol_out, res_out, dir_out, held, store_sem):
    own1 = layout(lax.axis_index("gx"), sizes["gx"])[1] + 1
    row = tail[0]
    gram = [[None] * DIM for _ in range(DIM)]
    for (i, j), k in SLOT.items():
        gram[i][j] = gram[j][i] = jnp.broadcast_to(row[:, k:k + 1], (8, 128))
    weights = coefficients(gram, tail[1], tail[2])
    tall = [[w if w is None else jnp.concatenate([w] * 4, axis=0) for w in entry] for entry in weights]
    stores = []
    for half in range(2):
        for x in range(4 * half, 4 * half + 4):
            sums = [sol_ref[x], None, None]
            for i in range(DIM):
                value = fields[TERMS[i], own1 + x, 8:40, :]
                for n in range(3):
                    if tall[n][i] is not None:
                        sums[n] = plus(sums[n], tall[n][i] * value)
            for n in range(3):
                held[n, x] = sums[n]
        layers = pl.ds(4 * half, 4)
        for n, out in enumerate((sol_out, res_out, dir_out)):
            stores.append(pltpu.make_async_copy(held.at[n, layers], out.at[layers], store_sem.at[3 * half + n]))
            stores[-1].start()
    for store in stores:
        store.wait()


def solution(mesh):
    sizes = {axis: mesh.shape[axis] for axis in AXES}
    total = sizes["gx"] * sizes["gy"] * sizes["gz"]
    stages = [AXES] if total <= 64 else [(axis,) for axis in AXES]
    rows = 0
    for axes in stages:
        members = 1
        for axis in axes:
            members *= sizes[axis]
        rows += members
    slots = 12 if sizes["gx"] == 2 else 16
    sides = 1 if sizes["gx"] == 2 else 2
    parts = message_count(sizes)
    nz = sizes["gz"]

    def body(sol, res, direction, material, cond_table, cap_table, gas, supply):
        hbm = pl.BlockSpec(memory_space=pltpu.HBM)
        f32 = jnp.float32
        block = jax.ShapeDtypeStruct((8, 32, 128), f32)
        dma = pltpu.SemaphoreType.DMA
        vmem = pl.BlockSpec(memory_space=pltpu.VMEM)
        kept = pl.pallas_call(
            lambda *refs: kernel(sizes, stages, *refs),
            out_shape=(
                jax.ShapeDtypeStruct((FIELDS, slots + 2, 48, 128), f32),
                jax.ShapeDtypeStruct((3, 8, 128), f32),
                block,
            ),
            in_specs=[hbm] * 8,
            out_specs=(vmem, vmem, vmem),
            scratch_shapes=[
                pltpu.VMEM((FIELDS, 48, 128), f32),
                pltpu.SMEM((8,), f32),
                pltpu.SMEM((8,), f32),
                pltpu.VMEM((8, 32, 128), jnp.int32),
                pltpu.VMEM((nz, 48, 128), f32),
                pltpu.VMEM((48, 128), jnp.int32),
                pltpu.VMEM((slots + 2, 48, 128), f32),
                pltpu.VMEM((slots, 40, 128), f32),
                pltpu.VMEM((slots + 1, 40, 128), f32),
                pltpu.VMEM((slots, 48, 128), f32),
                pltpu.VMEM((slots, 40, 128), f32),
                pltpu.VMEM((slots, 40, 128), f32),
                pltpu.VMEM((48, 128), f32),
                pltpu.VMEM((40, 128), f32),
                pltpu.VMEM((5, 40, 128), f32),
                pltpu.VMEM((48, 128), f32),
                pltpu.VMEM((5, 40, 128), f32),
                pltpu.VMEM((2, 4, 8, 128), f32),
                pltpu.VMEM((sides, 2, 4, 8, 128), f32),
                pltpu.VMEM((sides, 2, 16, 128), f32),
                pltpu.VMEM((2, 6, 8, 128), f32),
                pltpu.VMEM((sides, 2, 6, 8, 128), f32),
                pltpu.VMEM((sides, 2, 16, 128), f32),
                pltpu.VMEM((len(stages), 1, 128), f32),
                pltpu.VMEM((rows, 1, 128), f32),
                dma((parts,)),
                dma((parts,)),
                dma((3, nz)),
                dma((3, nz)),
                dma((2,)),
                dma((2,)),
                dma((rows,)),
                dma((rows,)),
                dma((8,)),
                pltpu.SemaphoreType.REGULAR((6,)),
            ],
            compiler_params=pltpu.CompilerParams(
                collective_id=0, has_side_effects=True, vmem_limit_bytes=VMEM // 2
            ),
            cost_estimate=pl.CostEstimate(flops=10**7, bytes_accessed=10**6, transcendentals=0),
        )(*[
            pltpu.with_memory_space_constraint(value, pltpu.HBM)
            for value in (cond_table, cap_table, sol, res, direction, material, gas, supply)
        ])
        return pl.pallas_call(
            lambda *refs: combine(sizes, *refs),
            out_shape=(block, block, block),
            in_specs=[vmem] * 3,
            out_specs=(hbm, hbm, hbm),
            scratch_shapes=[pltpu.VMEM((3, 8, 32, 128), f32), dma((6,))],
            compiler_params=pltpu.CompilerParams(vmem_limit_bytes=VMEM // 4),
        )(*kept)

    spec = P("gx", "gy", "gz")
    in_specs = (spec, spec, spec, spec, P(), P(), P("gy", "gz"), P("gy", "gz"))
    return jax.shard_map(
        body, mesh=mesh, in_specs=in_specs, out_specs=(spec, spec, spec), check_vma=False
    )
```

```python
import jax
import jax.numpy as jnp
from jax import lax
from jax.experimental import pallas as pl
from jax.experimental.pallas import tpu as pltpu
from jax.sharding import PartitionSpec as P

STEPS = 4
VMEM = 64 * 1024 * 1024
AXES = ("gx", "gy", "gz")
MESH = pl.DeviceIdType.MESH
DIM = 2 * STEPS + 1
PAIRS = [(i, j) for i in range(DIM) for j in range(i, DIM)]
SLOT = {pair: k for k, pair in enumerate(PAIRS)}


def harmonic(a, b):
    return 2.0 * a * b / jnp.maximum(a + b, 1e-30)


def tree(parts):
    while len(parts) > 1:
        parts = [sum(parts[k:k + 2][1:], parts[k]) for k in range(0, len(parts), 2)]
    return parts[0]


def times(a, b):
    return None if a is None or b is None else a * b


def plus(a, b):
    return b if a is None else a if b is None else a + b


def shift_product(p, center, half_width):
    q = [None] * DIM
    for offset, length in ((0, STEPS + 1), (STEPS + 1, STEPS)):
        for column in range(length - 1):
            entry = p[offset + column]
            if entry is None:
                continue
            q[offset + column] = plus(q[offset + column], center * entry)
            low = half_width if column == 0 else 0.5 * half_width
            q[offset + column + 1] = plus(q[offset + column + 1], low * entry)
            if column >= 1:
                q[offset + column - 1] = plus(q[offset + column - 1], 0.5 * half_width * entry)
    return q


def form(gram, a, b):
    total = None
    for i in range(DIM):
        if a[i] is None:
            continue
        row = None
        for j in range(DIM):
            row = plus(row, times(gram[i][j], b[j]))
        total = plus(total, a[i] * row)
    return total


def coefficients(gram, center, half_width):
    one = jnp.ones_like(gram[0][0])
    p = [None] * DIM
    r = [None] * DIM
    x = [None] * DIM
    p[0] = one
    r[STEPS + 1] = one
    rr = form(gram, r, r)
    for _ in range(STEPS):
        q = shift_product(p, center, half_width)
        step = rr / form(gram, p, q)
        x = [plus(x[i], times(step, p[i])) for i in range(DIM)]
        r = [plus(r[i], times(-step, q[i])) for i in range(DIM)]
        new = form(gram, r, r)
        ratio = new / rr
        p = [plus(r[i], times(ratio, p[i])) for i in range(DIM)]
        rr = new
    return x, r, p


MAT, D0, S0 = 0, 1, 2
TERMS = [D0, 3, 4, 5, 6, S0, 7, 8, 9]
FIELDS = 10


EDGE = []
for _field, _depth in ((MAT, 4), (D0, 4), (S0, 3)):
    for _i in range(1, _depth):
        EDGE.append((_field, _i, _depth - _i, sum(entry[2] for entry in EDGE)))


def both(*conditions):
    kept = [c for c in conditions if c is not True]
    if not kept:
        return True
    total = kept[0]
    for c in kept[1:]:
        total = jnp.logical_and(total, c)
    return total


def guard(condition, action):
    if condition is True:
        action()
    else:
        pl.when(condition)(action)


def layout(gx, count):
    if count == 2:
        own = 4 * gx
        sides = [dict(
            peer=1 - gx, send=True, recv=True, ghost=8 * (1 - gx),
            src4=4, dst4=8 * gx, in4=8 * (1 - gx),
            src3=5 - gx, dst3=1 + 7 * gx, in3=1 + 7 * (1 - gx),
            first=4 * (1 - gx), face=8 - 4 * gx, beside=7 - 3 * gx,
            near=lambda i: 8 - i + gx * (2 * i - 5), far=lambda i: 7 + i - gx * (2 * i + 3),
        )]
        return 12, own, sides
    own = 4
    sides = [
        dict(peer=gx - 1, send=gx > 0, recv=gx < count - 1, ghost=12,
             src4=4, dst4=12, in4=12, src3=4, dst3=12, in3=12, first=0, face=12, beside=11,
             near=lambda i: 3 + i, far=lambda i: 11 + i),
        dict(peer=gx + 1, send=gx < count - 1, recv=gx > 0, ghost=0,
             src4=8, dst4=0, in4=0, src3=9, dst3=1, in3=1, first=4, face=4, beside=4,
             near=lambda i: 12 - i, far=lambda i: 4 - i),
    ]
    return 16, own, sides


def message_count(sizes):
    sides = 1 if sizes["gx"] == 2 else 2
    return 8 + sides * 10


def kernel(
    sizes, stages, cond_in, cap_in, sol_in, res_in, dir_in, mat_in, gas_in, map_in,
    fields, tail, sol_ref,
    strip, cond_tab, cap_tab, mat_ref, flux, map_ref,
    condm, diag, kx, ky, kzl, kzh, kyc, kzc, conds, syc, sdiag, sk, sy, aside,
    pack, corner, edge, strip_in, corner_in, edge_in, gram_send, gram_halo,
    send_sem, recv_sem, flux_ssem, flux_rsem, map_ssem, map_rsem,
    gram_ssem, gram_rsem, load_sem, known,
):
    pos = {axis: lax.axis_index(axis) for axis in AXES}
    gx, gy, gz = (pos[axis] for axis in AXES)
    nx, ny, nz = (sizes[axis] for axis in AXES)
    slots, own, sides = layout(gx, nx)
    is_top = gx == nx - 1
    lane = lax.broadcasted_iota(jnp.int32, (8, 128), 1)
    group = lane // 8
    inner = lax.rem(lane, 8)
    own1 = own + 1

    loads = []
    for source, target in (
        (mat_in, mat_ref),
        (dir_in, fields.at[D0, pl.ds(own1, 8), pl.ds(8, 32)]),
        (res_in, fields.at[S0, pl.ds(own1, 8), pl.ds(8, 32)]),
        (map_in, map_ref.at[pl.ds(8, 32)]),
        (gas_in, flux.at[gz, pl.ds(8, 32)]),
        (cond_in, cond_tab), (cap_in, cap_tab),
        (sol_in, sol_ref),
    ):
        loads.append(pltpu.make_async_copy(source, target, load_sem.at[len(loads)]))
        loads[-1].start()

    barrier = pltpu.get_barrier_semaphore()
    count = jnp.int32(0)

    def inside(axis, step):
        if step == 0:
            return True
        return pos[axis] > 0 if step < 0 else pos[axis] < sizes[axis] - 1

    def greet(condition, peer):
        nonlocal count
        guard(condition, lambda: pl.semaphore_signal(barrier, inc=1, device_id=peer, device_id_type=MESH))
        count = count + (1 if condition is True else jnp.where(condition, 1, 0))

    def along(axis):
        return [lax.rem(pos[axis] + o, sizes[axis]) for o in range(1, sizes[axis])]

    for side in sides + [None]:
        for dy in (0, -1, 1):
            for dz in (0, -1, 1):
                if side is None and not dy and not dz:
                    continue
                peer = {"gy": gy + dy, "gz": gz + dz}
                if side is not None:
                    peer["gx"] = side["peer"]
                greet(
                    both(True if side is None else side["send"], inside("gy", dy), inside("gz", dz)), peer
                )

    def spread(number, axis, step=None, ask=True):
        n, p = sizes[axis], pos[axis]
        if step is None:
            for s in range(2, n - 2):
                spread(number, axis, s, False)
                spread(number, axis, s)
            return
        if step >= n - 2:
            return
        if not ask:
            for way, there, here in (
                (0, -1, jnp.logical_and(p >= 1, p + 1 + step <= n - 1)),
                (1, 1, jnp.logical_and(p <= n - 2, p - 1 - step >= 0)),
            ):
                guard(here, lambda: pl.semaphore_signal(
                    known.at[2 * number + way], inc=1, device_id={axis: p + there}, device_id_type=MESH))
            return
        for way, there in ((0, p + 2 + step <= n - 1), (1, p - 2 - step >= 0)):
            guard(there, lambda: pl.semaphore_wait(known.at[2 * number + way], 1))

    def blank(condition, slot_start, slot_count, rows):
        def fill():
            for f, value in ((MAT, -1.0), (D0, 0.0), (S0, 0.0)):
                fields[f, pl.ds(slot_start, slot_count), rows, :] = jnp.full(
                    (slot_count, rows.stop - rows.start, 128), value, jnp.float32
                )
        guard(condition, fill)

    low_rows, high_rows = slice(0, 8), slice(40, 48)
    blank(gy == 0, 1, slots, low_rows)
    blank(gy == ny - 1, 1, slots, high_rows)
    for side in sides:
        if side["recv"] is not True:
            blank(jnp.logical_not(side["recv"]), side["in4"] + 1, 4, slice(0, 48))
    zeros48 = jnp.zeros((48, 128), jnp.float32)
    for f in range(FIELDS):
        fields[f, 0] = zeros48
        fields[f, slots + 1] = zeros48
    condm[0] = zeros48
    condm[slots + 1] = zeros48
    kyc[...] = jnp.zeros((slots, 48, 128), jnp.float32)
    syc[...] = zeros48

    def blank_strip(condition, dz_index, rows):
        def fill():
            for k in rows:
                strip_in[dz_index, k] = jnp.where(lane < 32, -1.0, 0.0)
        guard(condition, fill)

    def blank_corner(condition, x_index, dz_index, rows):
        def fill():
            for k in rows:
                corner_in[x_index, dz_index, k] = jnp.where(lane < 16, -1.0, 0.0)
        guard(condition, fill)

    for dz_index, alone in ((0, gz == 0), (1, gz == nz - 1)):
        blank_strip(alone, dz_index, range(6))
        blank_strip(gy == 0, dz_index, [0])
        blank_strip(gy == ny - 1, dz_index, [5])
        for x_index, side in enumerate(sides):
            blank_corner(alone, x_index, dz_index, range(6))
            blank_corner(gy == 0, x_index, dz_index, [0])
            blank_corner(gy == ny - 1, x_index, dz_index, [5])
            if side["recv"] is not True:
                blank_corner(jnp.logical_not(side["recv"]), x_index, dz_index, range(6))

    def blank_flux(condition, rows):
        def fill():
            flux[:, rows, :] = jnp.zeros((nz, 8, 128), jnp.float32)
            map_ref[rows, :] = jnp.zeros((8, 128), jnp.int32)
        guard(condition, fill)

    blank_flux(gy == 0, low_rows)
    blank_flux(gy == ny - 1, high_rows)

    messages = []
    for x_index, side in [(None, None)] + list(enumerate(sides)):
        for dy in (-1, 0, 1):
            for dz in (-1, 0, 1):
                if side is None and not dy and not dz:
                    continue
                sends = both(inside("gy", dy), inside("gz", dz))
                takes = both(inside("gy", -dy), inside("gz", -dz))
                peer = {}
                if dy:
                    peer["gy"] = gy + dy
                if dz:
                    peer["gz"] = gz + dz
                if side is not None:
                    sends = both(sends, side["send"])
                    takes = both(takes, side["recv"])
                    peer["gx"] = side["peer"]
                row_from = pl.ds(8, 32) if not dy else pl.ds(32, 8) if dy > 0 else pl.ds(8, 8)
                row_to = pl.ds(8, 32) if not dy else pl.ds(0, 8) if dy > 0 else pl.ds(40, 8)
                tile_from = pl.ds(0, 4) if not dy else pl.ds(3, 1) if dy > 0 else pl.ds(0, 1)
                tile_to = pl.ds(1, 4) if not dy else pl.ds(0, 1) if dy > 0 else pl.ds(5, 1)
                came = 0 if dz > 0 else 1
                if side is None and not dz:
                    parts = [(
                        fields.at[pl.ds(0, 3), pl.ds(own1, 8), row_from],
                        fields.at[pl.ds(0, 3), pl.ds(own1, 8), row_to],
                        fields.at[pl.ds(0, 3), pl.ds(own1, 8), row_to],
                    )]
                elif side is None:
                    target = strip_in.at[came, tile_to]
                    parts = [(pack.at[came, tile_from], target, target)]
                elif dz:
                    target = corner_in.at[x_index, came, tile_to]
                    parts = [(corner.at[x_index, came, tile_from], target, target)]
                elif dy:
                    target = edge_in.at[x_index, (dy + 1) // 2]
                    parts = [(edge.at[x_index, (dy + 1) // 2], target, target)]
                else:
                    parts = [tuple(
                        fields.at[pl.ds(0, 2), pl.ds(side[name] + 1, 4), row_from]
                        for name in ("src4", "dst4", "in4")
                    ), tuple(
                        fields.at[S0, pl.ds(side[name] + 1, 3), row_from]
                        for name in ("src3", "dst3", "in3")
                    )]
                for part, (source, target, landing) in enumerate(parts):
                    number = len(messages)
                    messages.append(dict(
                        sends=sends, takes=takes, kind=(x_index, dy, dz), part=part,
                        copy=pltpu.make_async_remote_copy(
                            src_ref=source, dst_ref=target,
                            send_sem=send_sem.at[number], recv_sem=recv_sem.at[number],
                            device_id=peer, device_id_type=MESH,
                        ),
                        landed=pltpu.make_async_remote_copy(
                            src_ref=landing, dst_ref=landing,
                            send_sem=send_sem.at[number], recv_sem=recv_sem.at[number],
                            device_id=peer, device_id_type=MESH,
                        ),
                    ))

    wall = []
    for kind, dy in enumerate((0, -1, 1)):
        row_from = pl.ds(8, 32) if not dy else pl.ds(32, 8) if dy > 0 else pl.ds(8, 8)
        row_to = pl.ds(8, 32) if not dy else pl.ds(0, 8) if dy > 0 else pl.ds(40, 8)
        sends = both(is_top, inside("gy", dy))
        takes = both(is_top, inside("gy", -dy))
        if dy:
            wall.append(dict(
                sends=sends, takes=takes,
                copy=pltpu.make_async_remote_copy(
                    src_ref=map_ref.at[row_from], dst_ref=map_ref.at[row_to],
                    send_sem=map_ssem.at[kind - 1], recv_sem=map_rsem.at[kind - 1],
                    device_id={"gy": gy + dy}, device_id_type=MESH,
                ),
                landed=pltpu.make_async_remote_copy(
                    src_ref=map_ref.at[row_to], dst_ref=map_ref.at[row_to],
                    send_sem=map_ssem.at[kind - 1], recv_sem=map_rsem.at[kind - 1],
                    device_id={"gy": gy - dy}, device_id_type=MESH,
                ),
            ))
        for o in range(nz):
            if not dy and not o:
                continue
            z = lax.rem(gz + o, nz)
            peer = {"gy": gy + dy, "gz": z}
            wall.append(dict(
                sends=sends, takes=takes,
                copy=pltpu.make_async_remote_copy(
                    src_ref=flux.at[gz, row_from], dst_ref=flux.at[gz, row_to],
                    send_sem=flux_ssem.at[kind, z], recv_sem=flux_rsem.at[kind, gz],
                    device_id=peer, device_id_type=MESH,
                ),
                landed=pltpu.make_async_remote_copy(
                    src_ref=flux.at[z, row_to], dst_ref=flux.at[z, row_to],
                    send_sem=flux_ssem.at[kind, z], recv_sem=flux_rsem.at[kind, z],
                    device_id=peer, device_id_type=MESH,
                ),
            ))

    def start(test, part=None):
        for entry in messages:
            if test(*entry["kind"]) and part in (None, entry["part"]):
                guard(entry["sends"], entry["copy"].start)

    def finish(test, part=0):
        for entry in messages:
            if test(*entry["kind"]) and part == entry["part"]:
                guard(entry["takes"], entry["landed"].wait_recv)

    loads[0].wait()
    fields[MAT, pl.ds(own1, 8), pl.ds(8, 32), :] = mat_ref[...].astype(jnp.float32)
    loads[1].wait()
    loads[2].wait()
    pl.semaphore_wait(barrier, count)
    spread(0, "gz", 0, False)
    start(lambda x, y, z: x is not None and not y and not z, 0)
    start(lambda x, y, z: x is None and y and not z)

    for x_index, side in enumerate(sides):
        for which in range(2):
            for f, i, n, offset in EDGE:
                first = 40 - n if which else 8
                edge[x_index, which, offset:offset + n, :] = fields[f, side["near"](i) + 1, first:first + n, :]
    start(lambda x, y, z: x is not None and y and not z)

    loads[3].wait()
    for k in range(4):
        rows = slice(8 + 8 * k, 16 + 8 * k)
        wide = []
        for f in range(3):
            tile = jnp.zeros((8, 128), jnp.float32)
            for i in range(8):
                moved = pltpu.roll(fields[f, own1 + i, rows, :], 8 * i + 4, axis=1)
                tile = jnp.where(group == i, moved, tile)
            wide.append(tile)
        wide.append(pltpu.roll(map_ref[rows, :].astype(jnp.float32), 8 * 7 + 4, axis=1))
        for came in range(2):
            tile = jnp.zeros((8, 128), jnp.float32)
            source = 8 * (lax.rem(lane, 32) // 4) + lax.rem(lane, 4) + 4 * came
            for f in range(4):
                tile = jnp.where(lane // 32 == f, jnp.take_along_axis(wide[f], source, axis=1), tile)
            pack[came, k] = tile
            for x_index, side in enumerate(sides):
                tile = jnp.zeros((8, 128), jnp.float32)
                source = 8 * (lax.rem(lane, 16) // 4 + side["first"]) + lax.rem(lane, 4) + 4 * came
                for f in range(3):
                    tile = jnp.where(lane // 16 == f, jnp.take_along_axis(wide[f], source, axis=1), tile)
                corner[x_index, came, k] = tile
    start(lambda x, y, z: z and x is not None)
    start(lambda x, y, z: z and x is None)
    start(lambda x, y, z: x is not None and not y and not z, 1)
    spread(0, "gz", 0)
    spread(0, "gz", 1, False)

    loads[5].wait()
    loads[6].wait()
    cond_max, cap_max, cap_min = cond_tab[0], cap_tab[0], cap_tab[0]
    for m in range(1, 8):
        cond_max = jnp.maximum(cond_max, cond_tab[m])
        cap_max = jnp.maximum(cap_max, cap_tab[m])
        cap_min = jnp.minimum(cap_min, cap_tab[m])
    highest = cap_max + 12.0 * cond_max
    center = 0.5 * (highest + cap_min)
    half_width = jnp.full((8, 128), 0.5 * (highest - cap_min), jnp.float32)
    half40 = jnp.concatenate([half_width] * 5, axis=0)

    def lookup(material, table):
        value = jnp.zeros_like(material)
        for m in range(8):
            value = jnp.where(material == m, table[m], value)
        return value

    def tall(tile, rows):
        return jnp.concatenate([tile] * (rows // 8), axis=0)

    lane40 = tall(lane, 40)
    inner40 = tall(inner, 40)
    group40 = tall(group, 40)

    def span(first, value, otherwise, count):
        return jnp.where(jnp.logical_and(group >= first, group < first + count), value, otherwise)

    def join(k, f):
        source = 32 * f + 4 * jnp.clip(group - own, 0, 7) + 3 - lax.rem(inner, 4)
        high = jnp.take_along_axis(strip_in[1, k], source, axis=1)
        low = jnp.take_along_axis(strip_in[0, k], source, axis=1)
        return jnp.where(inner < 4, high, low)

    def join_corner(k, f, x_index):
        source = 16 * f + 4 * jnp.clip(group - sides[x_index]["ghost"], 0, 3) + 3 - lax.rem(inner, 4)
        high = jnp.take_along_axis(corner_in[x_index, 1, k], source, axis=1)
        low = jnp.take_along_axis(corner_in[x_index, 0, k], source, axis=1)
        return jnp.where(inner < 4, high, low)

    nothing = jnp.zeros((40, 128), jnp.float32)

    def collect(value_of, first, count):
        tile = nothing
        for i in range(count):
            tile = jnp.where(group40 == i, pltpu.roll(value_of(first + i), 8 * i + 4, axis=1), tile)
        if isinstance(first, int):
            return pltpu.roll(tile, 8 * first, axis=1) if first else tile
        return pltpu.roll(tile, lax.rem(8 * first, 128), axis=1)

    def strip_edges(source, first):
        tile = strip_cond() if source is None else strip[source, 4:44, :]
        if isinstance(first, int):
            return pltpu.roll(tile, (128 - 8 * first) % 128, axis=1) if first else tile
        return pltpu.roll(tile, lax.rem(128 - 8 * first, 128), axis=1)

    def strip_cond():
        return conds[4:44, :]

    ends40 = jnp.logical_or(lane40 == 0, lane40 == 127)
    sub = lax.broadcasted_iota(jnp.int32, (8, 128), 0)

    def y_faces(cond_ref, inside_ref, across_ref):
        across = []
        for r in range(4, 44, 8):
            low = harmonic(cond_ref[r - 1:r + 7, :], cond_ref[r:r + 8, :])
            if r in (4, 36):
                high = harmonic(cond_ref[r:r + 8, :], cond_ref[r + 1:r + 9, :])
                across.append(jnp.where(sub == 4, low, jnp.where(sub == 3, high, 0.0)))
                across_ref[r:r + 8, :] = across[-1]
                low = jnp.where(sub == 4, 0.0, low)
            inside_ref[r:r + 8, :] = low
        last = harmonic(cond_ref[39:47, :], cond_ref[40:48, :])
        inside_ref[40:48, :] = jnp.where(sub == 0, 0.0, last)
        return jnp.concatenate([across[0], jnp.zeros((24, 128), jnp.float32), across[1]], axis=0)

    def less_y_across(acc, across_ref, value_ref, row, height):
        parts = []
        for r in (row, row + height - 8):
            low, high = value_ref[r - 1:r + 7, :], value_ref[r + 1:r + 9, :]
            if row == 4:
                value = jnp.where(sub == 4, low, high)
            else:
                value = low if r == row else high
            at = r - row
            parts.append(acc[at:at + 8] - across_ref[r:r + 8, :] * value)
        return jnp.concatenate([parts[0], acc[8:height - 8], parts[1]], axis=0)

    def main_coefficients(first, count):
        edges = strip_edges(None, first)
        for i in range(count):
            at = first + i
            here = condm[at + 1, 4:44, :]
            edge_value = pltpu.roll(edges, 124 - 8 * i, axis=1)
            low = jnp.where(lane40 == 0, nothing, harmonic(pltpu.roll(here, 1, axis=1), here))
            high = jnp.where(lane40 == 127, nothing, harmonic(pltpu.roll(here, 127, axis=1), here))
            across = jnp.where(ends40, harmonic(jnp.where(ends40, edge_value, nothing), here), nothing)
            kzl[at] = low
            kzh[at] = high
            kzc[at] = across
            faces = y_faces(condm.at[at + 1], ky.at[at], kyc.at[at])
            cap = lookup(fields[MAT, at + 1, 4:44, :], cap_tab)
            diag[at] = (
                (cap - center) + ky[at, 4:44, :] + ky[at, 5:45, :] + low + high + kx[at] + kx[at + 1] + across
            ) + faces

    def strip_coefficients():
        cond_strip = strip_cond()
        sk[0] = jnp.where(jnp.logical_or(inner40 == 0, inner40 == 4), nothing, harmonic(pltpu.roll(cond_strip, 1, axis=1), cond_strip))
        sk[1] = jnp.where(jnp.logical_or(inner40 == 3, inner40 == 7), nothing, harmonic(pltpu.roll(cond_strip, 127, axis=1), cond_strip))
        low = harmonic(pltpu.roll(cond_strip, 8, axis=1), cond_strip)
        high = harmonic(pltpu.roll(cond_strip, 120, axis=1), cond_strip)
        if nx == 2:
            face = sides[0]["face"]
            sk[5] = jnp.where(group40 == face, low, jnp.where(group40 == face - 1, high, nothing))
            sk[2] = jnp.where(group40 == face, nothing, low)
            sk[3] = jnp.where(group40 == face - 1, nothing, high)
        else:
            sk[2] = low
            sk[3] = high
        sk[4] = jnp.where(jnp.logical_or(inner40 == 3, inner40 == 4), harmonic(aside[4], cond_strip), nothing)
        faces = y_faces(conds, sy, syc)
        sdiag[...] = (
            (lookup(strip[MAT, 4:44, :], cap_tab) - center)
            + sy[4:44, :] + sy[5:45, :] + sk[1] + sk[0] + low + high + sk[4]
        ) + faces

    def sweep(source, before, target, starts, count, last=False):
        first = starts[0] if starts[0] == starts[1] else starts[0] + (starts[1] - starts[0]) * gx
        face = sides[0]["face"]
        row, height = (8, 32) if last else (4, 40)
        edges = strip_edges(source, first)[row - 4:row - 4 + height]
        c = slice(row - 4, row - 4 + height)
        for i in range(count):
            at = first + i
            v = fields[source, at + 1, row:row + height, :]
            edge_value = pltpu.roll(edges, 124 - 8 * i, axis=1)
            k_low, k_high = kx[at, c, :], kx[at + 1, c, :]
            x_low = fields[source, at, row:row + height, :]
            x_high = fields[source, at + 2, row:row + height, :]
            low_last = nx == 2 and (starts[0] + i == 8 or starts[1] + i == 4)
            high_last = nx == 2 and (starts[0] + i == 7 or starts[1] + i == 3)
            acc = diag[at, c, :] * v
            acc = acc - (jnp.where(at == face, 0.0, k_low) if low_last else k_low) * x_low
            acc = acc - (jnp.where(at == face - 1, 0.0, k_high) if high_last else k_high) * x_high
            acc = acc - ky[at, row:row + height, :] * fields[source, at + 1, row - 1:row - 1 + height, :]
            acc = acc - ky[at, row + 1:row + 1 + height, :] * fields[source, at + 1, row + 1:row + 1 + height, :]
            acc = acc - kzl[at, c, :] * pltpu.roll(v, 1, axis=1) - kzh[at, c, :] * pltpu.roll(v, 127, axis=1)
            acc = acc - kzc[at, c, :] * jnp.where(ends40[:height], edge_value, 0.0)
            acc = less_y_across(acc, kyc.at[at], fields.at[source, at + 1], row, height)
            if low_last:
                acc = acc - jnp.where(at == face, k_low, 0.0) * x_low
            if high_last:
                acc = acc - jnp.where(at == face - 1, k_high, 0.0) * x_high
            acc = acc / half40[:height]
            if before is not None:
                acc = 2.0 * acc - fields[before, at + 1, row:row + height, :]
            fields[target, at + 1, row:row + height, :] = acc

    def sweep_strip(source, before, target, boundary):
        v = strip[source, 4:44, :]
        low, high = pltpu.roll(v, 8, axis=1), pltpu.roll(v, 120, axis=1)
        acc = sdiag[...] * v - sk[2] * low - sk[3] * high
        acc = acc - sy[4:44, :] * strip[source, 3:43, :] - sy[5:45, :] * strip[source, 5:45, :]
        acc = acc - sk[1] * pltpu.roll(v, 127, axis=1) - sk[0] * pltpu.roll(v, 1, axis=1)
        acc = acc - sk[4] * boundary
        acc = less_y_across(acc, syc, strip.at[source], 4, 40)
        if nx == 2:
            acc = acc - sk[5] * jnp.where(group40 == sides[0]["face"], low, high)
        acc = acc / half40
        if before is not None:
            acc = 2.0 * acc - strip[before, 4:44, :]
        strip[target, 4:44, :] = acc

    def main_of(f):
        return lambda at: fields[f, at + 1, 4:44, :]

    def chain(terms, degree):
        for t in range(1, degree + 1):
            shrink = STEPS - degree + t
            if nx == 2:
                starts, count = (0, shrink), 12 - shrink
            else:
                starts, count = (shrink, shrink), 16 - 2 * shrink
            if t == degree:
                starts, count = (0, 4) if nx == 2 else (4, 4), 8
            before = terms[t - 2] if t > 1 else None
            sweep(terms[t - 1], before, terms[t], starts, count, t == degree)
            if t < degree:
                sweep_strip(terms[t - 1], before, terms[t], collect(main_of(terms[t - 1]), 0, slots))

    def term(i):
        return fields[TERMS[i], pl.ds(own1, 8), pl.ds(8, 32), :].reshape(32, 8, 128)

    def gram_part(total, pairs):
        for i, j in pairs:
            product = term(i) * term(j)
            value = tree([tree([product[8 * a + g] for a in range(4)]) for g in range(8)])
            value = jnp.sum(value, axis=1, keepdims=True)
            total = jnp.where(lane == SLOT[(i, j)], value, total)
        return total

    def find(k, wanted):
        holder, index = wanted // 128, lax.rem(wanted, 128)
        value = jnp.zeros((8, 128), jnp.float32)
        for q in range(nz):
            found = jnp.take_along_axis(flux[q, 8 * k:8 * k + 8, :], index, axis=1)
            value = jnp.where(holder == q, found, value)
        return value

    def add_wall():
        for k in range(6):
            rows = slice(8 * k, 8 * k + 8)
            fields[S0, own1 + 7, rows, :] = fields[S0, own1 + 7, rows, :] + find(k, map_ref[rows, :])
            wanted = join(k, 3).astype(jnp.int32)
            strip[S0, rows, :] = strip[S0, rows, :] + jnp.where(group == own + 7, find(k, wanted), 0.0)

    direction = TERMS[:STEPS + 1]
    for i in range(8):
        condm[own1 + i, 8:40, :] = lookup(fields[MAT, own1 + i, 8:40, :], cond_tab)
    for i in range(1, 8):
        kx[own + i, 4:36, :] = harmonic(condm[own + i, 8:40, :], condm[own + i + 1, 8:40, :])
    loads[4].wait()
    spread(0, "gz", 1)
    spread(0, "gz")
    spread(1, "gy", 0, False)
    for entry in wall:
        guard(entry["sends"], entry["copy"].start)
    finish(lambda x, y, z: x is None)
    for k in range(6):
        for f in range(3):
            value = join(k, f)
            strip[f, 8 * k:8 * k + 8, :] = span(own, value, -1.0, 8) if f == MAT else value
    for i in range(8):
        for rows in (slice(0, 8), slice(40, 48)):
            condm[own1 + i, rows, :] = lookup(fields[MAT, own1 + i, rows, :], cond_tab)
    conds[...] = lookup(strip[MAT], cond_tab)
    kx[own] = nothing
    kx[own + 8] = nothing
    for i in range(1, 8):
        for r in (0, 32):
            low, high = condm[own + i, r + 4:r + 12, :], condm[own + i + 1, r + 4:r + 12, :]
            kx[own + i, r:r + 8, :] = harmonic(low, high)
    main_coefficients(own, 8)
    if nx == 2:
        aside[4] = collect(lambda at: condm[at + 1, 4:44, :], own, 8)
        strip_coefficients()
        for t in range(1, STEPS + 1):
            before = direction[t - 2] if t > 1 else None
            sweep(direction[t - 1], before, direction[t], (0, 4 + t), 8 - t, t == STEPS)
            aside[t - 1] = collect(main_of(direction[t - 1]), own, 8)
            if t < STEPS:
                sweep_strip(direction[t - 1], before, direction[t], aside[t - 1])

    spread(1, "gy", 0)
    spread(1, "gy", 1, False)
    finish(lambda x, y, z: x is not None)
    for x_index, side in enumerate(sides):
        for which in range(2):
            def unload():
                for f, i, n, offset in EDGE:
                    target = 8 - n if which else 40
                    fields[f, side["far"](i) + 1, target:target + n, :] = edge_in[x_index, which, offset:offset + n, :]
            guard(both(side["recv"], gy > 0 if which else gy < ny - 1), unload)
    for k in range(6):
        for x_index, side in enumerate(sides):
            for f in range(3):
                rows = slice(8 * k, 8 * k + 8)
                strip[f, rows, :] = span(side["ghost"], join_corner(k, f, x_index), strip[f, rows, :], 4)
    for side in sides:
        for g in range(4):
            condm[side["in4"] + g + 1] = lookup(fields[MAT, side["in4"] + g + 1], cond_tab)
    conds[...] = lookup(strip[MAT], cond_tab)
    aside[4] = collect(lambda at: condm[at + 1, 4:44, :], 0, slots)
    strip_coefficients()
    for side in sides:
        for g in range(5):
            at = side["in4"] + g
            kx[at] = harmonic(condm[at, 4:44, :], condm[at + 1, 4:44, :])
        main_coefficients(side["beside"], 1)
        main_coefficients(side["in4"], 4)
    if nx == 2:
        for t in range(1, STEPS + 1):
            before = direction[t - 2] if t > 1 else None
            sweep(direction[t - 1], before, direction[t], (8 - t, t), 4, t == STEPS)
            if t < STEPS:
                newer = 9 - t + (2 * t - 10) * gx
                fresh = collect(main_of(direction[t - 1]), newer, 4)
                hit = jnp.logical_and(group40 >= newer, group40 < newer + 4)
                sweep_strip(direction[t - 1], before, direction[t], jnp.where(hit, fresh, aside[t - 1]))
    else:
        chain(direction, STEPS)
    total = gram_part(jnp.zeros((8, 128), jnp.float32), [(i, j) for i, j in PAIRS if j <= STEPS])
    spread(1, "gy", 1)
    spread(1, "gy")
    for step in (0, 1):
        spread(2, "gx", step, False)
        spread(2, "gx", step)
    spread(2, "gx")

    finish(lambda x, y, z: True, 1)
    for entry in wall:
        guard(entry["takes"], entry["landed"].wait_recv)
    for entry in messages:
        guard(entry["sends"], entry["copy"].wait_send)
    pl.when(is_top)(add_wall)
    chain(TERMS[STEPS + 1:], STEPS - 1)
    total = gram_part(total, [(i, j) for i, j in PAIRS if j > STEPS])

    def peers(axes):
        found = [{}]
        for axis in axes:
            found = [dict(entry, **{axis: o}) for entry in found for o in range(sizes[axis])]
        found = [entry for entry in found if any(entry.values())]
        return [
            {axis: lax.rem(pos[axis] + o, sizes[axis]) for axis, o in entry.items()} for entry in found
        ]

    def index_of(axes, where):
        index = 0
        for axis in axes:
            index = index * sizes[axis] + where[axis]
        return index

    row = jnp.sum(total, axis=0, keepdims=True)
    base = 0
    gram_copies = []
    for stage, axes in enumerate(stages):
        members = 1
        for axis in axes:
            members *= sizes[axis]
        mine = base + index_of(axes, pos)
        gram_send[stage] = row
        gram_halo[mine] = row
        for peer in peers(axes):
            other = base + index_of(axes, peer)
            copy = pltpu.make_async_remote_copy(
                src_ref=gram_send.at[stage], dst_ref=gram_halo.at[mine],
                send_sem=gram_ssem.at[other], recv_sem=gram_rsem.at[mine],
                device_id=peer, device_id_type=MESH,
            )
            copy.start()
            gram_copies.append(copy)
        for peer in peers(axes):
            other = base + index_of(axes, peer)
            pltpu.make_async_remote_copy(
                src_ref=gram_halo.at[other], dst_ref=gram_halo.at[other],
                send_sem=gram_ssem.at[other], recv_sem=gram_rsem.at[other],
                device_id=peer, device_id_type=MESH,
            ).wait_recv()
        row = tree([gram_halo[base + member] for member in range(members)])
        base += members

    tail[0] = jnp.broadcast_to(row, (8, 128))
    tail[1] = jnp.full((8, 128), center, jnp.float32)
    tail[2] = half_width
    loads[7].wait()
    for entry in wall:
        guard(entry["sends"], entry["copy"].wait_send)
    for copy in gram_copies:
        copy.wait_send()


def combine(sizes, fields, tail, sol_ref, sol_out, res_out, dir_out, held, store_sem):
    own1 = layout(lax.axis_index("gx"), sizes["gx"])[1] + 1
    row = tail[0]
    gram = [[None] * DIM for _ in range(DIM)]
    for (i, j), k in SLOT.items():
        gram[i][j] = gram[j][i] = jnp.broadcast_to(row[:, k:k + 1], (8, 128))
    weights = coefficients(gram, tail[1], tail[2])
    tall = [[w if w is None else jnp.concatenate([w] * 4, axis=0) for w in entry] for entry in weights]
    stores = []
    for half in range(2):
        for x in range(4 * half, 4 * half + 4):
            sums = [sol_ref[x], None, None]
            for i in range(DIM):
                value = fields[TERMS[i], own1 + x, 8:40, :]
                for n in range(3):
                    if tall[n][i] is not None:
                        sums[n] = plus(sums[n], tall[n][i] * value)
            for n in range(3):
                held[n, x] = sums[n]
        layers = pl.ds(4 * half, 4)
        for n, out in enumerate((sol_out, res_out, dir_out)):
            stores.append(pltpu.make_async_copy(held.at[n, layers], out.at[layers], store_sem.at[3 * half + n]))
            stores[-1].start()
    for store in stores:
        store.wait()


def solution(mesh):
    sizes = {axis: mesh.shape[axis] for axis in AXES}
    total = sizes["gx"] * sizes["gy"] * sizes["gz"]
    stages = [AXES] if total <= 64 else [(axis,) for axis in AXES]
    rows = 0
    for axes in stages:
        members = 1
        for axis in axes:
            members *= sizes[axis]
        rows += members
    slots = 12 if sizes["gx"] == 2 else 16
    sides = 1 if sizes["gx"] == 2 else 2
    parts = message_count(sizes)
    nz = sizes["gz"]

    def body(sol, res, direction, material, cond_table, cap_table, gas, supply):
        hbm = pl.BlockSpec(memory_space=pltpu.HBM)
        f32 = jnp.float32
        block = jax.ShapeDtypeStruct((8, 32, 128), f32)
        dma = pltpu.SemaphoreType.DMA
        vmem = pl.BlockSpec(memory_space=pltpu.VMEM)
        kept = pl.pallas_call(
            lambda *refs: kernel(sizes, stages, *refs),
            out_shape=(
                jax.ShapeDtypeStruct((FIELDS, slots + 2, 48, 128), f32),
                jax.ShapeDtypeStruct((3, 8, 128), f32),
                block,
            ),
            in_specs=[hbm] * 8,
            out_specs=(vmem, vmem, vmem),
            scratch_shapes=[
                pltpu.VMEM((FIELDS, 48, 128), f32),
                pltpu.SMEM((8,), f32),
                pltpu.SMEM((8,), f32),
                pltpu.VMEM((8, 32, 128), jnp.int32),
                pltpu.VMEM((nz, 48, 128), f32),
                pltpu.VMEM((48, 128), jnp.int32),
                pltpu.VMEM((slots + 2, 48, 128), f32),
                pltpu.VMEM((slots, 40, 128), f32),
                pltpu.VMEM((slots + 1, 40, 128), f32),
                pltpu.VMEM((slots, 48, 128), f32),
                pltpu.VMEM((slots, 40, 128), f32),
                pltpu.VMEM((slots, 40, 128), f32),
                pltpu.VMEM((slots, 48, 128), f32),
                pltpu.VMEM((slots, 40, 128), f32),
                pltpu.VMEM((48, 128), f32),
                pltpu.VMEM((48, 128), f32),
                pltpu.VMEM((40, 128), f32),
                pltpu.VMEM((6, 40, 128), f32),
                pltpu.VMEM((48, 128), f32),
                pltpu.VMEM((5, 40, 128), f32),
                pltpu.VMEM((2, 4, 8, 128), f32),
                pltpu.VMEM((sides, 2, 4, 8, 128), f32),
                pltpu.VMEM((sides, 2, 16, 128), f32),
                pltpu.VMEM((2, 6, 8, 128), f32),
                pltpu.VMEM((sides, 2, 6, 8, 128), f32),
                pltpu.VMEM((sides, 2, 16, 128), f32),
                pltpu.VMEM((len(stages), 1, 128), f32),
                pltpu.VMEM((rows, 1, 128), f32),
                dma((parts,)),
                dma((parts,)),
                dma((3, nz)),
                dma((3, nz)),
                dma((2,)),
                dma((2,)),
                dma((rows,)),
                dma((rows,)),
                dma((8,)),
                pltpu.SemaphoreType.REGULAR((6,)),
            ],
            compiler_params=pltpu.CompilerParams(
                collective_id=0, has_side_effects=True, vmem_limit_bytes=VMEM // 2
            ),
            cost_estimate=pl.CostEstimate(flops=10**7, bytes_accessed=10**6, transcendentals=0),
        )(*[
            pltpu.with_memory_space_constraint(value, pltpu.HBM)
            for value in (cond_table, cap_table, sol, res, direction, material, gas, supply)
        ])
        return pl.pallas_call(
            lambda *refs: combine(sizes, *refs),
            out_shape=(block, block, block),
            in_specs=[vmem] * 3,
            out_specs=(hbm, hbm, hbm),
            scratch_shapes=[pltpu.VMEM((3, 8, 32, 128), f32), dma((6,))],
            compiler_params=pltpu.CompilerParams(vmem_limit_bytes=VMEM // 4),
        )(*kept)

    spec = P("gx", "gy", "gz")
    in_specs = (spec, spec, spec, spec, P(), P(), P("gy", "gz"), P("gy", "gz"))
    return jax.shard_map(
        body, mesh=mesh, in_specs=in_specs, out_specs=(spec, spec, spec), check_vma=False
    )
```
